32 devices in a mesh: grp: 2 (over y), res: 4 (over z), seq: 2 (over x), head: 2 (over core).
Axes of the slice: x: 2, y: 2, z: 4, core: 2. Of those that a mesh axis runs over, the one named last changes fastest.
Arguments:
- tokens: bfloat16 [24, 512, 768], P(('grp', 'seq'), 'res'), parts along dimension 0, may hold values from -20 to 20
- weights: int32 [24], P(('grp', 'seq')), parts along dimension 0, may hold values from 3 to 17
- key_mask: int32 [1024], P(('grp', 'res')), parts along dimension 0, may hold values 0 or 1
- w_query: bfloat16 [768, 768], P(None, 'head'), may hold values from -0.21875 to 0.21875
- w_key: bfloat16 [768, 768], P(None, 'head'), may hold values from -0.21875 to 0.21875
- w_value: bfloat16 [768, 768], P(None, 'head'), may hold values from -0.21875 to 0.21875
- w_out: bfloat16 [768, 768], P('head'), may hold values from -0.21875 to 0.21875
Outputs:
- attention_out: bfloat16 [24, 512, 768], P(('grp', 'seq'), 'res', 'head'), parts along dimension 0
The draws below stay inside these ranges and needn't reach their ends.
There are 2 independent parts, one for each index of `grp`. The reference program is written for one: setup_inputs(seed, part) draws one part's arguments, and reference() takes and returns one part's arrays. A program takes and returns all parts, laid end to end along the dimension named above; an argument that names none is the same for every part. Nothing has to cross between parts.
All inputs are finite; a program needn't handle non-finite values. No bound on the sum of `key_mask` on one device may be relied on, other than what follows from the above.
Results may differ from the reference program's by a relative error of at most 0.011.
The reference program's roundings to bfloat16 on the way (of `query`, `probs` and `attended`) count: a program that leaves them out, or rounds other values in their place, can miss the bound.
Values may be sent and summed in bfloat16 or wider, within the bound.
No kernel may reach another device: no remote copies, remote signals or barrier semaphores. Data moves between devices by JAX's collectives and lax.ppermute only.
A program may use at most 64 MiB of HBM per device.

```python
import math
import jax
import jax.numpy as jnp
from jax import lax

D = 768
HEADS = 12
HEAD_DIM = 64
ROWS = 12
LENGTH = 512


def draw_tokens(key, part):
    parts = jax.random.split(key, 1)
    return jnp.clip(jax.random.normal(parts[0], (ROWS, LENGTH, D), jnp.float32), -6.0, 6.0).astype(jnp.bfloat16)


def draw_weights(key, part):
    index = jnp.arange(ROWS, dtype=jnp.int32)
    base = 3 + 12 * index // ROWS
    extra = jax.random.randint(key, (ROWS,), 0, 4)
    extra = extra.at[0].set(0).at[ROWS - 1].set(3)
    return (base + extra).astype(jnp.int32)


def set_ends(entries, rng, smallest, largest):
    spot = [jax.random.randint(jax.random.fold_in(rng, axis), (), 0, length) for axis, length in enumerate(entries.shape)]
    main_axis = entries.shape.index(max(entries.shape))
    next_to = spot[:main_axis] + [(spot[main_axis] + 1) % entries.shape[main_axis]] + spot[main_axis + 1:]
    return entries.at[tuple(spot)].set(smallest).at[tuple(next_to)].set(largest)


def shard_levels(key, dims, shards, smallest, top_value):
    factor_of = 1.0
    for axis_at, blocks in shards:
        heights = jax.random.uniform(jax.random.fold_in(jax.random.fold_in(key, 6), axis_at), (blocks,), jnp.float32, smallest / len(shards), top_value / len(shards))
        factor_of = factor_of * jnp.repeat(jnp.exp(heights), dims[axis_at] // blocks).reshape((-1,) + (1,) * (len(dims) - 1 - axis_at))
    return factor_of


def centred(stream_key, dims, scale, reach, cuts=(), kind=jnp.bfloat16):
    values = jax.random.normal(stream_key, dims, jnp.float32) * scale
    if len(cuts) > 0:
        values = shard_levels(stream_key, dims, cuts, -0.22, 0.18) * values
    return jnp.clip(values, min=-reach, max=reach).astype(kind)


def setup_inputs(seed: int = 0, part: int = 0) -> dict:
    streams_of = jax.random.split(jax.random.key(seed), 8)
    own_keys = jax.random.split(jax.random.fold_in(streams_of[7], part), 8)
    tokens = draw_tokens(jax.random.fold_in(jax.random.fold_in(streams_of[7], part), 71), part)
    weights = draw_weights(jax.random.fold_in(jax.random.fold_in(streams_of[7], part), 71), part)
    key_mask = set_ends((jax.random.randint(own_keys[2], (LENGTH,), 0, 8) < 7).astype(jnp.int32), jax.random.fold_in(own_keys[2], 1), 0, 1)
    w_query = centred(streams_of[3], (D, D), D ** -0.5, 0.21875, ((1, 2),))
    w_key = centred(streams_of[4], (D, D), D ** -0.5, 0.21875, ((1, 2),))
    w_value = centred(streams_of[5], (D, D), D ** -0.5, 0.21875, ((1, 2),))
    w_out = centred(streams_of[6], (D, D), D ** -0.5, 0.21875, ((0, 2),))
    return dict(tokens=tokens, weights=weights, key_mask=key_mask, w_query=w_query, w_key=w_key, w_value=w_value, w_out=w_out)


def reference(tokens, weights, key_mask, w_query, w_key, w_value, w_out):
    rows, cells, width = tokens.shape
    flat = tokens.reshape(rows * cells, width)
    total = jnp.sum(weights).astype(jnp.float32)
    factor = weights.astype(jnp.float32) * lax.rsqrt(total) / math.sqrt(HEAD_DIM)
    query = jnp.dot(flat, w_query, preferred_element_type=jnp.float32).reshape(rows, cells, HEADS, HEAD_DIM)
    query = (query * factor[:, None, None, None]).astype(jnp.bfloat16)
    keys = jnp.dot(flat, w_key, preferred_element_type=jnp.float32).astype(jnp.bfloat16).reshape(rows, cells, HEADS, HEAD_DIM)
    values = jnp.dot(flat, w_value, preferred_element_type=jnp.float32).astype(jnp.bfloat16).reshape(rows, cells, HEADS, HEAD_DIM)
    live = key_mask > 0

    def one_head(packed):
        q_head, k_head, v_head = packed
        logits = jnp.einsum('rie,rje->ij', q_head.astype(jnp.float32), k_head.astype(jnp.float32))
        logits = jnp.where(live[None, :], logits, -1000000000.0)
        top = lax.optimization_barrier(jnp.max(logits, axis=-1))
        expo = jnp.exp(logits - top[:, None])
        denom = lax.optimization_barrier(jnp.sum(expo, axis=-1))
        probs = expo.astype(jnp.bfloat16)
        summed = jnp.einsum('ij,rje->rie', probs.astype(jnp.float32), v_head.astype(jnp.float32))
        return (summed / denom[None, :, None]).astype(jnp.bfloat16)
    moved = (jnp.transpose(query, (2, 0, 1, 3)), jnp.transpose(keys, (2, 0, 1, 3)), jnp.transpose(values, (2, 0, 1, 3)))
    attended = lax.map(one_head, moved)
    attended = jnp.transpose(attended, (1, 2, 0, 3)).reshape(rows * cells, HEADS * HEAD_DIM)
    result = jnp.dot(attended, w_out, preferred_element_type=jnp.float32).astype(jnp.bfloat16)
    return result.reshape(rows, cells, width)
```

```python
import functools
import math

import jax
import jax.numpy as jnp
from jax import lax
from jax.experimental import pallas as pl
from jax.experimental.pallas import tpu as pltpu
from jax.sharding import PartitionSpec as P

HEAD_DIM = 64
LANES = 128
PER_TILE = LANES // HEAD_DIM
MASKED = -1000000000.0
VMEM_LIMIT = 24 * 1024 * 1024


def ring(value, axis, by=1):
    length = lax.axis_size(axis)
    return lax.ppermute(value, axis, [(i, (i + by) % length) for i in range(length)])


def whole(count):
    return [pl.BlockSpec(memory_space=pltpu.VMEM) for _ in range(count)]


def call(kernel, out_shape, args, flops, scalars=0, scratch=()):
    specs = [pl.BlockSpec(memory_space=pltpu.SMEM)] * scalars + whole(len(args) - scalars)
    multiple = isinstance(out_shape, (list, tuple))
    size = sum(a.size * a.dtype.itemsize for a in args)
    return pl.pallas_call(
        kernel,
        out_shape=out_shape,
        in_specs=specs,
        out_specs=whole(len(out_shape)) if multiple else whole(1)[0],
        scratch_shapes=list(scratch),
        cost_estimate=pl.CostEstimate(flops=int(flops), transcendentals=0, bytes_accessed=int(size)),
        compiler_params=pltpu.CompilerParams(vmem_limit_bytes=VMEM_LIMIT),
    )(*args)


def lane_head(shape):
    return lax.broadcasted_iota(jnp.int32, shape, len(shape) - 1) // HEAD_DIM


def dot(a, b):
    return jnp.dot(a, b, preferred_element_type=jnp.float32)


def dot_nt(a, b):
    return lax.dot_general(a, b, (((1,), (1,)), ((), ())), preferred_element_type=jnp.float32)


def per_head(value, pick):
    heads = lane_head(value.shape)
    parts = [pick(value, heads == h) for h in range(PER_TILE)]
    out = parts[-1]
    for h in range(PER_TILE - 2, -1, -1):
        out = jnp.where(heads == h, parts[h], out)
    return jnp.broadcast_to(out, value.shape)


def max_over(value, keep):
    return jnp.max(jnp.where(keep, value, -jnp.inf), axis=-1, keepdims=True)


def sum_over(value, keep):
    return jnp.sum(jnp.where(keep, value, 0.0), axis=-1, keepdims=True)


def spread(target, chunk, flat, first_row, cells):
    rows = flat.shape[0] // cells
    tiles = flat.shape[1] // LANES
    heads = lane_head((cells, LANES))
    for tile in range(tiles):
        for row in range(rows):
            part = flat[row * cells : (row + 1) * cells, tile * LANES : (tile + 1) * LANES]
            at = slice((first_row + row) * LANES, (first_row + row + 1) * LANES)
            for h in range(PER_TILE):
                kept = jnp.where(heads == h, part, jnp.zeros_like(part))
                target[chunk, tile, h * cells : (h + 1) * cells, at] = kept


def project_kernel(*refs, chunks, pieces):
    query, w_key, w_value = refs[:3]
    tokens = refs[3 : 3 + chunks * pieces]
    logits, values, keys = refs[3 + chunks * pieces :]
    rows, cells, width = tokens[0].shape
    for chunk in range(chunks):
        for piece in range(pieces):
            flat = tokens[chunk * pieces + piece][...].reshape(rows * cells, width)
            spread(keys, 0, dot(flat, w_key[...]).astype(jnp.bfloat16), piece * rows, cells)
            spread(values, chunk, dot(flat, w_value[...]).astype(jnp.bfloat16), piece * rows, cells)
        for tile in range(query.shape[0]):
            logits[chunk, tile] = dot_nt(query[tile], keys[0, tile])


def own_kernel(order, factor, tokens, w_query, w_key, w_value, query, logits, values, keys):
    rows, cells, width = tokens.shape
    chunks = logits.shape[0]
    part = cells // chunks
    for row in range(rows):
        source = order[row]
        block = tokens[source]
        scaled = (dot(block, w_query[...]) * factor[source]).astype(jnp.bfloat16)
        for tile in range(query.shape[0]):
            query[tile, :, row * LANES : (row + 1) * LANES] = scaled[:, tile * LANES : (tile + 1) * LANES]
        key = dot(block, w_key[...]).astype(jnp.bfloat16)
        value = dot(block, w_value[...]).astype(jnp.bfloat16)
        for chunk in range(chunks):
            spread(keys, chunk, key[chunk * part : (chunk + 1) * part], row, part)
            spread(values, chunk, value[chunk * part : (chunk + 1) * part], row, part)
    for chunk in range(chunks):
        for tile in range(query.shape[0]):
            logits[chunk, tile] = dot_nt(query[tile], keys[chunk, tile])


def absorb(units, state, tile, rows):
    scores, mixed = [], []
    for tiles, mask, values in units:
        for chunk in range(tiles[0].shape[0]):
            total = tiles[0][chunk, tile]
            for other in tiles[1:]:
                total = total + other[chunk, tile]
            scores.append(jnp.where(mask[chunk : chunk + 1] > 0, total, MASKED))
            mixed.append(values[chunk, tile])
    top = functools.reduce(jnp.maximum, scores)
    top = per_head(top, max_over)
    if state is not None:
        before = state[0][tile]
        top = jnp.maximum(top, before)
        rescale = jnp.exp(before - top)
    expo = [jnp.exp(score - top) for score in scores]
    denom = functools.reduce(jnp.add, expo)
    probs = jnp.concatenate([e.astype(jnp.bfloat16) for e in expo], axis=1)
    accum = dot(probs, jnp.concatenate(mixed, axis=0))
    if state is not None:
        denom = denom + state[1][tile] * rescale
        accum = accum + state[2][tile] * jnp.concatenate([rescale] * rows, axis=1)
    return top, denom, accum


def read_units(refs, sizes):
    units, at = [], 0
    for size in sizes:
        units.append((refs[at : at + size], refs[at + size], refs[at + size + 1]))
        at += size + 2
    return units, refs[at:]


def absorb_kernel(*refs, sizes, carried):
    units, refs = read_units(refs, sizes)
    state = refs[:3] if carried else None
    top, denom, accum = refs[-3:]
    rows = accum.shape[2] // LANES
    for tile in range(accum.shape[0]):
        top[tile], denom[tile], accum[tile] = absorb(units, state, tile, rows)


def finish_kernel(order, *refs, sizes, carried):
    units, refs = read_units(refs, sizes)
    state = refs[:3] if carried else None
    w_send, attended, sent = refs[-3:]
    rows, cells, _ = attended.shape
    for tile in range(attended.shape[2] // LANES):
        top, denom, accum = absorb(units, state, tile, rows)
        denom = per_head(denom, sum_over)
        for row in range(rows):
            part = accum[:, row * LANES : (row + 1) * LANES] / denom
            attended[row, :, tile * LANES : (tile + 1) * LANES] = part.astype(jnp.bfloat16)
    for row in range(rows):
        sent[order[row]] = dot(attended[row], w_send[...]).astype(jnp.bfloat16)


def output_kernel(order, attended, w_own, kept):
    for row in range(attended.shape[0]):
        kept[order[row]] = dot(attended[row], w_own[...])


def shards(tokens, weights, key_mask, w_query, w_key, w_value, w_out):
    rows, cells, width = tokens.shape
    inner = w_query.shape[1]
    tiles = inner // LANES
    blocks = lax.axis_size("res")
    holders = lax.axis_size("seq")
    cores = lax.axis_size("head")
    core = lax.axis_index("head")
    part = HEAD_DIM
    chunks = cells // part
    share = rows // cores
    assert share * cores == rows and chunks * part == cells and tiles * LANES == inner
    f32, bf16 = jnp.float32, jnp.bfloat16

    def shape(dims, kind):
        return jax.ShapeDtypeStruct(dims, kind)

    moving = [
        lax.dynamic_slice(tokens, (core * share, k * part, 0), (share, part, width))
        for k in range(chunks)
    ]
    mask = jnp.tile(key_mask.reshape(chunks, part), (1, PER_TILE))
    order = jnp.concatenate(
        [(core - k) % cores * share + jnp.arange(share, dtype=jnp.int32) for k in range(cores)]
    )

    total = jnp.full((8, LANES), jnp.sum(weights).astype(f32))
    passing = total
    for _ in range(holders - 1):
        passing = ring(passing, "seq")
        total = total + passing
    factor = weights.astype(f32) * lax.rsqrt(total[0, 0]) / math.sqrt(HEAD_DIM)

    def exchange(logits):
        return [logits] + [ring(logits, "seq", k) for k in range(1, holders)]

    depth = PER_TILE * part
    spans = rows * LANES
    query, logits, values = call(
        own_kernel,
        [
            shape((tiles, cells, spans), bf16),
            shape((chunks, tiles, cells, depth), f32),
            shape((chunks, tiles, depth, spans), bf16),
        ],
        [order, factor, tokens, w_query, w_key, w_value],
        2 * rows * cells * inner * (3 * width + cells * PER_TILE),
        scalars=2,
        scratch=[pltpu.VMEM((chunks, tiles, depth, spans), bf16)],
    )
    units = [(exchange(logits), mask, values)]

    def project(pieces, count):
        return call(
            functools.partial(project_kernel, chunks=count, pieces=cores),
            [shape((count, tiles, cells, depth), f32), shape((count, tiles, depth, spans), bf16)],
            [query, w_key, w_value] + pieces,
            2 * rows * part * count * inner * (2 * width + cells * PER_TILE),
            scratch=[pltpu.VMEM((1, tiles, depth, spans), bf16)],
        )

    for step in range(1, blocks):
        moving = [ring(piece, "res") for piece in moving]
        mask = ring(mask, "res")
        pieces = [[piece] + [ring(piece, "head", k) for k in range(1, cores)] for piece in moving]
        if step < blocks - 1:
            logits, values = project(sum(pieces, []), chunks)
            units.append((exchange(logits), mask, values))
        else:
            for k in range(chunks):
                logits, values = project(pieces[k], 1)
                units.append((exchange(logits), mask[k : k + 1], values))

    state = []
    state_shape = [
        shape((tiles, cells, LANES), f32),
        shape((tiles, cells, LANES), f32),
        shape((tiles, cells, spans), f32),
    ]

    def flatten(group):
        return sum([list(u[0]) + [u[1], u[2]] for u in group], [])

    def work(group):
        return sum(2 * u[0][0].size * spans for u in group)

    groups = []
    early = units[: len(units) - chunks] if blocks > 1 else []
    for at in range(0, len(early), 3):
        groups.append(early[at : at + 3])
    groups += [[unit] for unit in units[len(early) :]]
    for group in groups[:-1]:
        state = call(
            functools.partial(absorb_kernel, sizes=[len(u[0]) for u in group], carried=bool(state)),
            state_shape,
            flatten(group) + list(state),
            work(group),
        )
    group = groups[-1]
    columns = width // cores
    outs = [
        lax.dynamic_slice(w_out, (0, (core + k) % cores * columns), (inner, columns))
        for k in range(cores)
    ]
    attended, sent = call(
        functools.partial(finish_kernel, sizes=[len(u[0]) for u in group], carried=bool(state)),
        [shape((rows, cells, inner), bf16), shape((rows, cells, columns), bf16)],
        [order] + flatten(group) + list(state) + [outs[1 % cores]],
        work(group) + 2 * rows * cells * inner * columns,
        scalars=1,
    )

    def output(w):
        return call(
            output_kernel,
            shape((rows, cells, columns), f32),
            [order, attended, w],
            2 * rows * cells * inner * columns,
            scalars=1,
        )

    if cores == 1:
        return output(outs[0]).astype(bf16)
    received = [ring(sent, "head")]
    for k in range(2, cores):
        received.append(ring(output(outs[k]).astype(bf16), "head", k))
    result = output(outs[0])
    for value in received:
        result = result + value.astype(f32)
    return result.astype(bf16)


def solution(mesh):
    in_specs = (
        P(("grp", "seq"), "res", None),
        P(("grp", "seq")),
        P(("grp", "res")),
        P(None, "head"),
        P(None, "head"),
        P(None, "head"),
        P("head", None),
    )
    out_specs = P(("grp", "seq"), "res", "head")
    return jax.shard_map(shards, mesh=mesh, in_specs=in_specs, out_specs=out_specs, check_vma=False)
```

```python
import functools
import math

import jax
import jax.numpy as jnp
from jax import lax
from jax.experimental import pallas as pl
from jax.experimental.pallas import tpu as pltpu
from jax.sharding import PartitionSpec as P


HEAD_DIM = 64
LANES = 128
PER_TILE = LANES // HEAD_DIM
CHUNKS = 2
MASKED = -1000000000.0
VMEM_LIMIT = 24 * 1024 * 1024


def ring(value, axis, by=1):
    length = lax.axis_size(axis)
    return lax.ppermute(value, axis, [(i, (i + by) % length) for i in range(length)])


def whole(count):
    return [pl.BlockSpec(memory_space=pltpu.VMEM) for _ in range(count)]


def call(kernel, out_shape, args, flops, scalars=0, scratch=()):
    specs = [pl.BlockSpec(memory_space=pltpu.SMEM)] * scalars + whole(len(args) - scalars)
    multiple = isinstance(out_shape, (list, tuple))
    size = sum(a.size * a.dtype.itemsize for a in args)
    return pl.pallas_call(
        kernel,
        out_shape=out_shape,
        in_specs=specs,
        out_specs=whole(len(out_shape)) if multiple else whole(1)[0],
        scratch_shapes=list(scratch),
        cost_estimate=pl.CostEstimate(flops=int(flops), transcendentals=0, bytes_accessed=int(size)),
        compiler_params=pltpu.CompilerParams(vmem_limit_bytes=VMEM_LIMIT),
    )(*args)


def lane_head(shape):
    return lax.broadcasted_iota(jnp.int32, shape, len(shape) - 1) // HEAD_DIM


def dot(a, b):
    return jnp.dot(a, b, preferred_element_type=jnp.float32)


def dot_nt(a, b):
    return lax.dot_general(a, b, (((1,), (1,)), ((), ())), preferred_element_type=jnp.float32)


def per_head(value, pick):
    heads = lane_head(value.shape)
    parts = [pick(value, heads == h) for h in range(PER_TILE)]
    out = parts[-1]
    for h in range(PER_TILE - 2, -1, -1):
        out = jnp.where(heads == h, parts[h], out)
    return jnp.broadcast_to(out, value.shape)


def max_over(value, keep):
    return jnp.max(jnp.where(keep, value, -jnp.inf), axis=-1, keepdims=True)


def sum_over(value, keep):
    return jnp.sum(jnp.where(keep, value, 0.0), axis=-1, keepdims=True)


def spread(target, chunk, flat, first_row, cells):
    rows = flat.shape[0] // cells
    tiles = flat.shape[1] // LANES
    heads = lane_head((cells, LANES))
    for tile in range(tiles):
        for row in range(rows):
            part = flat[row * cells : (row + 1) * cells, tile * LANES : (tile + 1) * LANES]
            at = slice((first_row + row) * LANES, (first_row + row + 1) * LANES)
            for h in range(PER_TILE):
                kept = jnp.where(heads == h, part, jnp.zeros_like(part))
                target[chunk, tile, h * cells : (h + 1) * cells, at] = kept


def project_kernel(*refs, chunks, pieces):
    query, w_key, w_value = refs[:3]
    tokens = refs[3 : 3 + chunks * pieces]
    logits, values, keys = refs[3 + chunks * pieces :]
    rows, cells, width = tokens[0].shape
    for chunk in range(chunks):
        for piece in range(pieces):
            flat = tokens[chunk * pieces + piece][...].reshape(rows * cells, width)
            spread(keys, 0, dot(flat, w_key[...]).astype(jnp.bfloat16), piece * rows, cells)
            spread(values, chunk, dot(flat, w_value[...]).astype(jnp.bfloat16), piece * rows, cells)
        for tile in range(query.shape[0]):
            logits[chunk, tile] = dot_nt(query[tile], keys[0, tile])


def own_kernel(order, *refs):
    counts, refs = refs[:-8], refs[-8:]
    tokens, w_query, w_key, w_value, query, logits, values, keys = refs
    rows, cells, _ = tokens.shape
    chunks = logits.shape[0]
    part = cells // chunks
    total = sum(count[row] for count in counts for row in range(rows))
    scale = lax.rsqrt(jnp.full((1, query.shape[0] * LANES), total, jnp.int32).astype(jnp.float32))
    for row in range(rows):
        source = order[row]
        block = tokens[source]
        count = jnp.full(scale.shape, counts[0][source], jnp.int32).astype(jnp.float32)
        factor = count * scale / math.sqrt(HEAD_DIM)
        scaled = (dot(block, w_query[...]) * factor).astype(jnp.bfloat16)
        for tile in range(query.shape[0]):
            query[tile, :, row * LANES : (row + 1) * LANES] = scaled[:, tile * LANES : (tile + 1) * LANES]
        key = dot(block, w_key[...]).astype(jnp.bfloat16)
        value = dot(block, w_value[...]).astype(jnp.bfloat16)
        for chunk in range(chunks):
            spread(keys, chunk, key[chunk * part : (chunk + 1) * part], row, part)
            spread(values, chunk, value[chunk * part : (chunk + 1) * part], row, part)
    for chunk in range(chunks):
        for tile in range(query.shape[0]):
            logits[chunk, tile] = dot_nt(query[tile], keys[chunk, tile])


def absorb(units, state, tile, rows):
    scores, mixed = [], []
    for tiles, mask, values in units:
        for chunk in range(tiles[0].shape[0]):
            total = tiles[0][chunk, tile]
            for other in tiles[1:]:
                total = total + other[chunk, tile]
            scores.append(jnp.where(mask[chunk : chunk + 1] > 0, total, MASKED))
            mixed.append(values[chunk, tile])
    top = functools.reduce(jnp.maximum, scores)
    top = per_head(top, max_over)
    if state is not None:
        before = state[0][tile]
        top = jnp.maximum(top, before)
        rescale = jnp.exp(before - top)
    expo = [jnp.exp(score - top) for score in scores]
    denom = functools.reduce(jnp.add, expo)
    probs = jnp.concatenate([e.astype(jnp.bfloat16) for e in expo], axis=1)
    accum = dot(probs, jnp.concatenate(mixed, axis=0))
    if state is not None:
        denom = denom + state[1][tile] * rescale
        accum = accum + state[2][tile] * jnp.concatenate([rescale] * rows, axis=1)
    return top, denom, accum


def read_units(refs, sizes):
    units, at = [], 0
    for size in sizes:
        units.append((refs[at : at + size], refs[at + size], refs[at + size + 1]))
        at += size + 2
    return units, refs[at:]


def absorb_kernel(*refs, sizes, carried):
    units, refs = read_units(refs, sizes)
    state = refs[:3] if carried else None
    top, denom, accum = refs[-3:]
    rows = accum.shape[2] // LANES
    for tile in range(accum.shape[0]):
        top[tile], denom[tile], accum[tile] = absorb(units, state, tile, rows)


def finish_kernel(order, *refs, sizes, carried):
    units, refs = read_units(refs, sizes)
    state = refs[:3] if carried else None
    w_send, attended, sent = refs[-3:]
    rows, _, _ = attended.shape
    for tile in range(attended.shape[2] // LANES):
        _, denom, accum = absorb(units, state, tile, rows)
        denom = per_head(denom, sum_over)
        for row in range(rows):
            part = accum[:, row * LANES : (row + 1) * LANES] / denom
            attended[row, :, tile * LANES : (tile + 1) * LANES] = part.astype(jnp.bfloat16)
    for row in range(rows):
        sent[order[row]] = dot(attended[row], w_send[...]).astype(jnp.bfloat16)


def output_kernel(order, attended, w_own, kept):
    for row in range(attended.shape[0]):
        kept[order[row]] = dot(attended[row], w_own[...])


def shards(tokens, weights, key_mask, w_query, w_key, w_value, w_out):
    rows, cells, width = tokens.shape
    inner = w_query.shape[1]
    tiles = inner // LANES
    blocks = lax.axis_size("res")
    holders = lax.axis_size("seq")
    cores = lax.axis_size("head")
    core = lax.axis_index("head")
    part = HEAD_DIM
    chunks = cells // part
    assert chunks == CHUNKS
    share = rows // cores
    assert share * cores == rows and chunks * part == cells and tiles * LANES == inner
    f32, bf16 = jnp.float32, jnp.bfloat16

    def shape(dims, kind):
        return jax.ShapeDtypeStruct(dims, kind)

    moving = [
        lax.dynamic_slice(tokens, (core * share, k * part, 0), (share, part, width))
        for k in range(chunks)
    ]
    mask = jnp.tile(key_mask.reshape(chunks, part), (1, PER_TILE))
    order = jnp.concatenate(
        [(core - k) % cores * share + jnp.arange(share, dtype=jnp.int32) for k in range(cores)]
    )

    counts = [weights]
    for k in range(1, holders):
        counts.append(ring(weights, "seq", k))

    def exchange(logits):
        return [logits] + [ring(logits, "seq", k) for k in range(1, holders)]

    depth = PER_TILE * part
    spans = rows * LANES
    query, logits, values = call(
        own_kernel,
        [
            shape((tiles, cells, spans), bf16),
            shape((chunks, tiles, cells, depth), f32),
            shape((chunks, tiles, depth, spans), bf16),
        ],
        [order] + counts + [tokens, w_query, w_key, w_value],
        2 * rows * cells * inner * (3 * width + cells * PER_TILE),
        1 + holders,
        [pltpu.VMEM((chunks, tiles, depth, spans), bf16)],
    )
    units = [(exchange(logits), mask, values)]

    def project(pieces):
        return call(
            functools.partial(project_kernel, chunks=1, pieces=cores),
            [shape((1, tiles, cells, depth), f32), shape((1, tiles, depth, spans), bf16)],
            [query, w_key, w_value] + pieces,
            2 * rows * part * inner * (2 * width + cells * PER_TILE),
            0,
            [pltpu.VMEM((1, tiles, depth, spans), bf16)],
        )

    for _ in range(1, blocks):
        moving = [ring(moving[k], "res") for k in range(chunks)]
        mask = ring(mask, "res")
        for k in range(chunks):
            pieces = [moving[k]]
            for j in range(1, cores):
                pieces.append(ring(moving[k], "head", j))
            logits, values = project(pieces)
            units.append((exchange(logits), mask[k : k + 1], values))

    state = []
    state_shape = [
        shape((tiles, cells, LANES), f32),
        shape((tiles, cells, LANES), f32),
        shape((tiles, cells, spans), f32),
    ]

    def flatten(group):
        return sum([list(u[0]) + [u[1], u[2]] for u in group], [])

    def work(group):
        return sum(2 * u[0][0].size * spans for u in group)

    groups = [units[at : at + 3] for at in range(0, len(units) - 1, 3)] + [units[-1:]]
    for group in groups[:-1]:
        state = call(
            functools.partial(absorb_kernel, sizes=[len(u[0]) for u in group], carried=bool(state)),
            state_shape,
            flatten(group) + list(state),
            work(group),
        )
    group = groups[-1]
    columns = width // cores
    outs = [
        lax.dynamic_slice(w_out, (0, (core + k) % cores * columns), (inner, columns))
        for k in range(cores)
    ]
    attended, sent = call(
        functools.partial(finish_kernel, sizes=[len(u[0]) for u in group], carried=bool(state)),
        [shape((rows, cells, inner), bf16), shape((rows, cells, columns), bf16)],
        [order] + flatten(group) + list(state) + [outs[1 % cores]],
        work(group) + 2 * rows * cells * inner * columns,
        1,
    )

    def output(w):
        return call(
            output_kernel,
            shape((rows, cells, columns), f32),
            [order, attended, w],
            2 * rows * cells * inner * columns,
            1,
        )

    if cores == 1:
        return output(outs[0]).astype(bf16)
    received = [ring(sent, "head")]
    for k in range(2, cores):
        received.append(ring(output(outs[k]).astype(bf16), "head", k))
    result = output(outs[0])
    for value in received:
        result = result + value.astype(f32)
    return result.astype(bf16)


def solution(mesh):
    in_specs = (
        P(("grp", "seq"), "res", None),
        P(("grp", "seq")),
        P(("grp", "res")),
        P(None, "head"),
        P(None, "head"),
        P(None, "head"),
        P("head", None),
    )
    out_specs = P(("grp", "seq"), "res", "head")

    return jax.shard_map(shards, mesh=mesh, in_specs=in_specs, out_specs=out_specs, check_vma=False)
```

```python
import functools
import math

import jax
import jax.numpy as jnp
from jax import lax
from jax.experimental import pallas as pl
from jax.experimental.pallas import tpu as pltpu
from jax.sharding import PartitionSpec as P


HEAD_DIM = 64
LANES = 128
PER_TILE = LANES // HEAD_DIM
CHUNKS = 2
MARK_ROWS = 16
MASKED = -1000000000.0
VMEM_LIMIT = 24 * 1024 * 1024


def ring(value, axis, by=1):
    length = lax.axis_size(axis)
    return lax.ppermute(value, axis, [(i, (i + by) % length) for i in range(length)])


def whole(count):
    return [pl.BlockSpec(memory_space=pltpu.VMEM) for _ in range(count)]


def call(kernel, out_shape, args, flops, scalars=0, scratch=()):
    specs = [pl.BlockSpec(memory_space=pltpu.SMEM)] * scalars + whole(len(args) - scalars)
    multiple = isinstance(out_shape, (list, tuple))
    size = sum(a.size * a.dtype.itemsize for a in args)
    return pl.pallas_call(
        kernel,
        out_shape=out_shape,
        in_specs=specs,
        out_specs=whole(len(out_shape)) if multiple else whole(1)[0],
        scratch_shapes=list(scratch),
        cost_estimate=pl.CostEstimate(flops=int(flops), transcendentals=0, bytes_accessed=int(size)),
        compiler_params=pltpu.CompilerParams(vmem_limit_bytes=VMEM_LIMIT),
    )(*args)


def lane_head(shape):
    return lax.broadcasted_iota(jnp.int32, shape, len(shape) - 1) // HEAD_DIM


def dot(a, b):
    return jnp.dot(a, b, preferred_element_type=jnp.float32)


def dot_nt(a, b):
    return lax.dot_general(a, b, (((1,), (1,)), ((), ())), preferred_element_type=jnp.float32)


def per_head(value, pick):
    heads = lane_head(value.shape)
    parts = [pick(value, heads == h) for h in range(PER_TILE)]
    out = parts[-1]
    for h in range(PER_TILE - 2, -1, -1):
        out = jnp.where(heads == h, parts[h], out)
    return jnp.broadcast_to(out, value.shape)


def max_over(value, keep):
    return jnp.max(jnp.where(keep, value, -jnp.inf), axis=-1, keepdims=True)


def sum_over(value, keep):
    return jnp.sum(jnp.where(keep, value, 0.0), axis=-1, keepdims=True)


def spread(target, chunk, flat, first_row, cells):
    rows = flat.shape[0] // cells
    tiles = flat.shape[1] // LANES
    heads = lane_head((cells, LANES))
    for tile in range(tiles):
        for row in range(rows):
            part = flat[row * cells : (row + 1) * cells, tile * LANES : (tile + 1) * LANES]
            at = slice((first_row + row) * LANES, (first_row + row + 1) * LANES)
            for h in range(PER_TILE):
                kept = jnp.where(heads == h, part, jnp.zeros_like(part))
                target[chunk, tile, h * cells : (h + 1) * cells, at] = kept


def own_row(row, share, cores):
    core = lax.axis_index("head")
    return lax.rem(core + (cores - row // share), cores) * share + row % share


def live_lanes(mask, chunk):
    turned = pltpu.roll(mask, HEAD_DIM, 1)
    first = lane_head(mask.shape) == 0
    return (jnp.where(first, mask, turned) if chunk == 0 else jnp.where(first, turned, mask))[:1] > 0


def score(query, keys, live, masked):
    return jnp.where(live, dot_nt(query, keys), masked)


def pack_kernel(tokens, mask, packed, landing, done, *, chunk, share):
    _, part, width = landing.shape
    core = lax.axis_index("head")
    copy = pltpu.make_async_copy(
        tokens.at[pl.ds(core * share, share), pl.ds(chunk * part, part)], landing, done
    )
    copy.start()
    size = share * part
    tail = packed.shape[0] - width // LANES * size
    packed[width // LANES * size :] = jnp.broadcast_to(
        mask[...].astype(jnp.float32), (tail, LANES)
    ).astype(jnp.bfloat16)
    copy.wait()
    for tile in range(width // LANES):
        at = slice(tile * LANES, (tile + 1) * LANES)
        packed[tile * size : (tile + 1) * size] = landing[:, :, at].reshape(size, LANES)


def unpack(packed, width, size):
    return jnp.concatenate(
        [packed[tile * size : (tile + 1) * size] for tile in range(width // LANES)], axis=1
    )


def project_kernel(*refs, order, masked):
    query, w_key, w_value = refs[:3]
    pieces = refs[3:-3]
    logits, values, keys = refs[-3:]
    tiles, width = query.shape[0], w_key.shape[0]
    chunks = len(order)
    per_chunk = len(pieces) // chunks
    part = keys.shape[2] // PER_TILE
    size = (pieces[0].shape[0] - MARK_ROWS) * LANES // width
    for at in range(chunks):
        own = pieces[at * per_chunk : (at + 1) * per_chunk]
        flat = jnp.concatenate([unpack(piece, width, size) for piece in own], axis=0)
        spread(keys, 0, dot(flat, w_key[...]).astype(jnp.bfloat16), 0, part)
        mask = own[0][own[0].shape[0] - MARK_ROWS :].astype(jnp.float32)
        live = live_lanes(mask[:8], order[at])
        for tile in range(tiles):
            logits[at, tile] = score(query[tile], keys[0, tile], live, masked)
        spread(values, at, dot(flat, w_value[...]).astype(jnp.bfloat16), 0, part)


def own_kernel(*refs, cores, masked):
    counts, refs = refs[:-9], refs[-9:]
    mask, tokens, w_query, w_key, w_value, query, logits, values, keys = refs
    rows, cells, _ = tokens.shape
    chunks = logits.shape[0]
    part = cells // chunks
    total = sum(count[row] for count in counts for row in range(rows))
    scale = lax.rsqrt(jnp.full((1, query.shape[0] * LANES), total, jnp.int32).astype(jnp.float32))
    for row in range(rows):
        source = own_row(row, rows // cores, cores)
        block = tokens[source]
        count = jnp.full(scale.shape, counts[0][source], jnp.int32).astype(jnp.float32)
        factor = count * scale / math.sqrt(HEAD_DIM)
        scaled = (dot(block, w_query[...]) * factor).astype(jnp.bfloat16)
        for tile in range(query.shape[0]):
            query[tile, :, row * LANES : (row + 1) * LANES] = scaled[:, tile * LANES : (tile + 1) * LANES]
        key = dot(block, w_key[...]).astype(jnp.bfloat16)
        value = dot(block, w_value[...]).astype(jnp.bfloat16)
        for chunk in range(chunks):
            spread(keys, chunk, key[chunk * part : (chunk + 1) * part], row, part)
            spread(values, chunk, value[chunk * part : (chunk + 1) * part], row, part)
    marks = jnp.broadcast_to(mask[...].astype(jnp.float32), (8, LANES))
    for chunk in range(chunks):
        live = live_lanes(marks, chunk)
        for tile in range(query.shape[0]):
            logits[chunk, tile] = score(query[tile], keys[chunk, tile], live, masked)


def absorb(units, state, tile, rows):
    scores, mixed = [], []
    for tiles, values in units:
        for chunk in range(tiles[0].shape[0]):
            total = tiles[0][chunk, tile]
            for other in tiles[1:]:
                total = total + other[chunk, tile]
            scores.append(total)
            mixed.append(values[chunk, tile])
    top = functools.reduce(jnp.maximum, scores)
    top = per_head(top, max_over)
    if state is not None:
        before = state[0][tile]
        top = jnp.maximum(top, before)
        rescale = jnp.exp(before - top)
    expo = [jnp.exp(score - top) for score in scores]
    denom = functools.reduce(jnp.add, expo)
    probs = jnp.concatenate([e.astype(jnp.bfloat16) for e in expo], axis=1)
    accum = dot(probs, jnp.concatenate(mixed, axis=0))
    if state is not None:
        denom = denom + state[1][tile] * rescale
        accum = accum + state[2][tile] * jnp.concatenate([rescale] * rows, axis=1)
    return top, denom, accum


def read_units(refs, sizes):
    units, at = [], 0
    for size in sizes:
        units.append((refs[at : at + size], refs[at + size]))
        at += size + 1
    return units, refs[at:]


def absorb_kernel(*refs, sizes, carried):
    units, refs = read_units(refs, sizes)
    state = refs[:3] if carried else None
    top, denom, accum = refs[-3:]
    rows = accum.shape[2] // LANES
    for tile in range(accum.shape[0]):
        top[tile], denom[tile], accum[tile] = absorb(units, state, tile, rows)


def columns_of(w_out, ahead, cores):
    columns = w_out.shape[1] // cores
    at = lax.rem(lax.axis_index("head") + ahead, cores) * columns
    return w_out[:, pl.ds(pl.multiple_of(at, LANES), columns)]


def finish_kernel(*refs, sizes, carried, cores):
    units, refs = read_units(refs, sizes)
    state = refs[:3] if carried else None
    w_out, attended, sent = refs[-3:]
    rows, _, _ = attended.shape
    for tile in range(attended.shape[2] // LANES):
        _, denom, accum = absorb(units, state, tile, rows)
        denom = per_head(denom, sum_over)
        for row in range(rows):
            part = accum[:, row * LANES : (row + 1) * LANES] / denom
            attended[row, :, tile * LANES : (tile + 1) * LANES] = part.astype(jnp.bfloat16)
    write_output(attended, columns_of(w_out, 1 % cores, cores), sent, cores)


def write_output(attended, w, target, cores):
    rows = attended.shape[0]
    for row in range(rows):
        target[own_row(row, rows // cores, cores)] = dot(attended[row], w).astype(target.dtype)


def output_kernel(attended, w_out, kept, *, ahead, cores):
    write_output(attended, columns_of(w_out, ahead, cores), kept, cores)


def batches(blocks):
    every = tuple(range(CHUNKS))
    out = []
    for step in range(1, blocks):
        if step < blocks - 2:
            out.append((step, every))
        else:
            out += [(step, (k,)) for k in every]
    return out


def shards(tokens, weights, key_mask, w_query, w_key, w_value, w_out):
    rows, cells, width = tokens.shape
    inner = w_query.shape[1]
    tiles = inner // LANES
    blocks = lax.axis_size("res")
    holders = lax.axis_size("seq")
    cores = lax.axis_size("head")
    part = HEAD_DIM
    share = rows // cores
    assert share * cores == rows and tiles * LANES == inner and part * CHUNKS == cells == LANES
    f32, bf16 = jnp.float32, jnp.bfloat16
    masked = MASKED / holders
    shape = pltpu.VMEM
    key_mask = key_mask.reshape(1, cells)

    length = share * part * width // LANES + MARK_ROWS
    moving = [
        pl.pallas_call(
            functools.partial(pack_kernel, chunk=k, share=share),
            out_shape=shape((length, LANES), bf16),
            in_specs=[pl.BlockSpec(memory_space=pl.ANY)] + whole(1),
            out_specs=whole(1)[0],
            scratch_shapes=[shape((share, part, width), bf16), pltpu.SemaphoreType.DMA],
            compiler_params=pltpu.CompilerParams(vmem_limit_bytes=VMEM_LIMIT),
        )(tokens, key_mask)
        for k in range(CHUNKS)
    ]
    counts = [weights]
    for k in range(1, holders):
        counts.append(ring(weights, "seq", k))

    def exchange(logits):
        return [logits] + [ring(logits, "seq", k) for k in range(1, holders)]

    depth = PER_TILE * part
    spans = rows * LANES
    query, logits, values = call(
        functools.partial(own_kernel, cores=cores, masked=masked),
        [
            shape((tiles, cells, spans), bf16),
            shape((CHUNKS, tiles, cells, depth), f32),
            shape((CHUNKS, tiles, depth, spans), bf16),
        ],
        counts + [key_mask, tokens, w_query, w_key, w_value],
        2 * rows * cells * inner * (3 * width + cells * PER_TILE),
        holders,
        [pltpu.VMEM((CHUNKS, tiles, depth, spans), bf16)],
    )
    units = [(exchange(logits), values)]

    pieces = {}
    for step in range(1, blocks):
        moving = [ring(moving[k], "res") for k in range(CHUNKS)]
        for k in range(CHUNKS):
            pieces[step, k] = [moving[k]] + [ring(moving[k], "head", j) for j in range(1, cores)]
    for step, taken in batches(blocks):
        count = len(taken)
        logits, values = call(
            functools.partial(project_kernel, order=taken, masked=masked),
            [shape((count, tiles, cells, depth), f32), shape((count, tiles, depth, spans), bf16)],
            [query, w_key, w_value] + sum([pieces[step, k] for k in taken], []),
            2 * rows * part * count * inner * (2 * width + cells * PER_TILE),
            0,
            [pltpu.VMEM((1, tiles, depth, spans), bf16)],
        )
        units.append((exchange(logits), values))

    state = []
    state_shape = [
        shape((tiles, cells, LANES), f32),
        shape((tiles, cells, LANES), f32),
        shape((tiles, cells, spans), f32),
    ]

    def flatten(group):
        return sum([list(u[0]) + [u[1]] for u in group], [])

    def work(group):
        return sum(2 * u[0][0].size * spans for u in group)

    cuts = groups_of(len(units))
    for cut in cuts[:-1]:
        group = units[slice(*cut)]
        state = call(
            functools.partial(absorb_kernel, sizes=[len(u[0]) for u in group], carried=bool(state)),
            state_shape,
            flatten(group) + list(state),
            work(group),
        )
    group = units[slice(*cuts[-1])]
    columns = width // cores
    attended, sent = call(
        functools.partial(
            finish_kernel, sizes=[len(u[0]) for u in group], carried=bool(state), cores=cores
        ),
        [shape((rows, cells, inner), bf16), shape((rows, cells, columns), bf16)],
        flatten(group) + list(state) + [w_out],
        work(group) + 2 * rows * cells * inner * columns,
    )

    def output(k):
        return call(
            functools.partial(output_kernel, ahead=k, cores=cores),
            shape((rows, cells, columns), f32),
            [attended, w_out],
            2 * rows * cells * inner * columns,
        )

    if cores == 1:
        return sent
    received = [ring(sent, "head")]
    for k in range(2, cores):
        received.append(ring(output(k).astype(bf16), "head", k))
    result = output(0)
    for value in received:
        result = result + value.astype(f32)
    return result.astype(bf16)


def groups_of(count):
    return [(at, min(at + 3, count - 1)) for at in range(0, count - 1, 3)] + [(count - 1, count)]


def solution(mesh):
    in_specs = (
        P(("grp", "seq"), "res", None),
        P(("grp", "seq")),
        P(("grp", "res")),
        P(None, "head"),
        P(None, "head"),
        P(None, "head"),
        P("head", None),
    )
    out_specs = P(("grp", "seq"), "res", "head")

    return jax.shard_map(shards, mesh=mesh, in_specs=in_specs, out_specs=out_specs, check_vma=False)
```

```python
import functools
import math

import jax
import jax.numpy as jnp
from jax import lax
from jax.experimental import pallas as pl
from jax.experimental.pallas import tpu as pltpu
from jax.sharding import PartitionSpec as P


HEAD_DIM = 64
LANES = 128
PER_TILE = LANES // HEAD_DIM
CHUNKS = 2
MARK_ROWS = 8
MASKED = -1000000000.0
VMEM_LIMIT = 24 * 1024 * 1024


def ring(value, axis, by=1):
    length = lax.axis_size(axis)
    return lax.ppermute(value, axis, [(i, (i + by) % length) for i in range(length)])


def whole(count):
    return [pl.BlockSpec(memory_space=pltpu.VMEM) for _ in range(count)]


def call(kernel, out_shape, args, flops, scalars=0, scratch=()):
    specs = [pl.BlockSpec(memory_space=pltpu.SMEM)] * scalars + whole(len(args) - scalars)
    multiple = isinstance(out_shape, (list, tuple))
    size = sum(a.size * a.dtype.itemsize for a in args)
    return pl.pallas_call(
        kernel,
        out_shape=out_shape,
        in_specs=specs,
        out_specs=whole(len(out_shape)) if multiple else whole(1)[0],
        scratch_shapes=list(scratch),
        cost_estimate=pl.CostEstimate(flops=int(flops), transcendentals=0, bytes_accessed=int(size)),
        compiler_params=pltpu.CompilerParams(vmem_limit_bytes=VMEM_LIMIT),
    )(*args)


def lane_head(shape):
    return lax.broadcasted_iota(jnp.int32, shape, len(shape) - 1) // HEAD_DIM


def dot(a, b):
    return jnp.dot(a, b, preferred_element_type=jnp.float32)


def dot_nt(a, b):
    return lax.dot_general(a, b, (((1,), (1,)), ((), ())), preferred_element_type=jnp.float32)


def per_head(value, pick):
    heads = lane_head(value.shape)
    parts = [pick(value, heads == h) for h in range(PER_TILE)]
    out = parts[-1]
    for h in range(PER_TILE - 2, -1, -1):
        out = jnp.where(heads == h, parts[h], out)
    return jnp.broadcast_to(out, value.shape)


def max_over(value, keep):
    return jnp.max(jnp.where(keep, value, -jnp.inf), axis=-1, keepdims=True)


def sum_over(value, keep):
    return jnp.sum(jnp.where(keep, value, 0.0), axis=-1, keepdims=True)


def spread(target, chunk, flat, first_row, cells):
    rows = flat.shape[0] // cells
    tiles = flat.shape[1] // LANES
    heads = lane_head((cells, LANES))
    for tile in range(tiles):
        for row in range(rows):
            part = flat[row * cells : (row + 1) * cells, tile * LANES : (tile + 1) * LANES]
            at = slice((first_row + row) * LANES, (first_row + row + 1) * LANES)
            for h in range(PER_TILE):
                kept = jnp.where(heads == h, part, jnp.zeros_like(part))
                target[chunk, tile, h * cells : (h + 1) * cells, at] = kept


def own_row(row, share, cores):
    core = lax.axis_index("head")
    return lax.rem(core + (cores - row // share), cores) * share + row % share


def live_lanes(mask, chunk):
    turned = pltpu.roll(mask, HEAD_DIM, 1)
    first = lane_head(mask.shape) == 0
    return (jnp.where(first, mask, turned) if chunk == 0 else jnp.where(first, turned, mask))[:1] > 0


def score(query, keys, live, masked):
    return jnp.where(live, dot_nt(query, keys), masked)


def pack_kernel(tokens, mask, packed, landing, marks, done, *, chunk, share):
    _, part, width = landing.shape
    core = lax.axis_index("head")
    size = share * part
    used = width // LANES * size
    copies = [
        pltpu.make_async_copy(
            tokens.at[pl.ds(core * share, share), pl.ds(chunk * part, part)], landing, done.at[0]
        )
    ]
    if packed.shape[0] > used:
        copies.append(pltpu.make_async_copy(mask, marks, done.at[1]))
    for copy in copies:
        copy.start()
    for copy in copies:
        copy.wait()
    for tile in range(width // LANES):
        at = slice(tile * LANES, (tile + 1) * LANES)
        packed[tile * size : (tile + 1) * size] = landing[:, :, at].reshape(size, LANES)
    if packed.shape[0] > used:
        tail = packed.shape[0] - used
        packed[used:] = jnp.broadcast_to(marks[...].astype(jnp.float32), (tail, LANES)).astype(jnp.bfloat16)


def unpack(pieces, width):
    tiles = width // LANES
    flats = []
    for piece in pieces:
        size = piece.shape[0] // tiles // HEAD_DIM * HEAD_DIM
        flats.append(
            jnp.concatenate([piece[tile * size : (tile + 1) * size] for tile in range(tiles)], axis=1)
        )
    return jnp.concatenate(flats, axis=0)


def marks_of(piece):
    return piece[piece.shape[0] - MARK_ROWS :].astype(jnp.float32)


def project_kernel(*refs, order, masked):
    query, w_key, w_value = refs[:3]
    pieces = refs[3:-3]
    logits, values, keys = refs[-3:]
    width = w_key.shape[0]
    per_chunk = len(pieces) // len(order)
    part = keys.shape[2] // PER_TILE
    for at, chunk in enumerate(order):
        flat = unpack(pieces[at * per_chunk : (at + 1) * per_chunk], width)
        spread(keys, 0, dot(flat, w_key[...]).astype(jnp.bfloat16), 0, part)
        live = live_lanes(marks_of(pieces[0]), chunk)
        for tile in range(query.shape[0]):
            logits[at, tile] = score(query[tile], keys[0, tile], live, masked)
        spread(values, at, dot(flat, w_value[...]).astype(jnp.bfloat16), 0, part)


def early_kernel(query, w_key, piece, logits, keys):
    spread(keys, 0, dot(unpack([piece], w_key.shape[0]), w_key[...]).astype(jnp.bfloat16), 0, HEAD_DIM)
    for tile in range(query.shape[0]):
        logits[0, tile] = dot_nt(query[tile, :, : keys.shape[3]], keys[0, tile])


def late_kernel(query, w_key, marks, before, *refs, chunk, masked):
    pieces, (logits, keys) = refs[:-2], refs[-2:]
    flat = unpack(pieces, w_key.shape[0])
    spread(keys, 0, dot(flat, w_key[...]).astype(jnp.bfloat16), 0, HEAD_DIM)
    live = live_lanes(marks_of(marks), chunk)
    skip = query.shape[2] - keys.shape[3]
    for tile in range(query.shape[0]):
        total = before[0, tile] + dot_nt(query[tile, :, skip:], keys[0, tile])
        logits[0, tile] = jnp.where(live, total, masked)


def values_kernel(w_value, *refs):
    pieces, values = refs[:-1], refs[-1]
    flat = unpack(pieces, w_value.shape[0])
    spread(values, 0, dot(flat, w_value[...]).astype(jnp.bfloat16), 0, HEAD_DIM)


def own_kernel(*refs, cores, masked):
    counts, refs = refs[:-9], refs[-9:]
    mask, tokens, w_query, w_key, w_value, query, logits, values, keys = refs
    rows, cells, _ = tokens.shape
    chunks = logits.shape[0]
    part = cells // chunks
    total = sum(count[row] for count in counts for row in range(rows))
    scale = lax.rsqrt(jnp.full((1, query.shape[0] * LANES), total, jnp.int32).astype(jnp.float32))
    for row in range(rows):
        source = own_row(row, rows // cores, cores)
        block = tokens[source]
        count = jnp.full(scale.shape, counts[0][source], jnp.int32).astype(jnp.float32)
        factor = count * scale / math.sqrt(HEAD_DIM)
        scaled = (dot(block, w_query[...]) * factor).astype(jnp.bfloat16)
        for tile in range(query.shape[0]):
            query[tile, :, row * LANES : (row + 1) * LANES] = scaled[:, tile * LANES : (tile + 1) * LANES]
        key = dot(block, w_key[...]).astype(jnp.bfloat16)
        value = dot(block, w_value[...]).astype(jnp.bfloat16)
        for chunk in range(chunks):
            spread(keys, chunk, key[chunk * part : (chunk + 1) * part], row, part)
            spread(values, chunk, value[chunk * part : (chunk + 1) * part], row, part)
    marks = jnp.broadcast_to(mask[...].astype(jnp.float32), (8, LANES))
    for chunk in range(chunks):
        live = live_lanes(marks, chunk)
        for tile in range(query.shape[0]):
            logits[chunk, tile] = score(query[tile], keys[chunk, tile], live, masked)


def absorb(units, state, tile, rows):
    scores, mixed = [], []
    for tiles, values in units:
        for chunk in range(tiles[0].shape[0]):
            total = tiles[0][chunk, tile]
            for other in tiles[1:]:
                total = total + other[chunk, tile]
            scores.append(total)
            mixed.append(values[chunk, tile])
    top = functools.reduce(jnp.maximum, scores)
    top = per_head(top, max_over)
    if state is not None:
        before = state[0][tile]
        top = jnp.maximum(top, before)
        rescale = jnp.exp(before - top)
    expo = [jnp.exp(score - top) for score in scores]
    denom = functools.reduce(jnp.add, expo)
    probs = jnp.concatenate([e.astype(jnp.bfloat16) for e in expo], axis=1)
    accum = dot(probs, jnp.concatenate(mixed, axis=0))
    if state is not None:
        denom = denom + state[1][tile] * rescale
        accum = accum + state[2][tile] * jnp.concatenate([rescale] * rows, axis=1)
    return top, denom, accum


def read_units(refs, sizes):
    units, at = [], 0
    for size in sizes:
        units.append((refs[at : at + size], refs[at + size]))
        at += size + 1
    return units, refs[at:]


def absorb_kernel(*refs, sizes, carried):
    units, refs = read_units(refs, sizes)
    state = refs[:3] if carried else None
    top, denom, accum = refs[-3:]
    rows = accum.shape[2] // LANES
    for tile in range(accum.shape[0]):
        top[tile], denom[tile], accum[tile] = absorb(units, state, tile, rows)


def columns_of(w_out, ahead, cores):
    columns = w_out.shape[1] // cores
    at = lax.rem(lax.axis_index("head") + ahead, cores) * columns
    return w_out[:, pl.ds(pl.multiple_of(at, LANES), columns)]


def finish_kernel(*refs, sizes, carried, cores):
    units, refs = read_units(refs, sizes)
    state = refs[:3] if carried else None
    w_out, attended, sent = refs[-3:]
    rows, _, _ = attended.shape
    for tile in range(attended.shape[2] // LANES):
        _, denom, accum = absorb(units, state, tile, rows)
        denom = per_head(denom, sum_over)
        for row in range(rows):
            part = accum[:, row * LANES : (row + 1) * LANES] / denom
            attended[row, :, tile * LANES : (tile + 1) * LANES] = part.astype(jnp.bfloat16)
    write_output(attended, columns_of(w_out, 1 % cores, cores), sent, cores)


def write_output(attended, w, target, cores):
    rows = attended.shape[0]
    for row in range(rows):
        target[own_row(row, rows // cores, cores)] = dot(attended[row], w).astype(target.dtype)


def output_kernel(attended, w_out, kept, *, ahead, cores):
    write_output(attended, columns_of(w_out, ahead, cores), kept, cores)


def batches(blocks):
    every = tuple(range(CHUNKS))
    out = []
    for step in range(1, blocks):
        if step < blocks - 2:
            out.append((step, every))
        else:
            out += [(step, (k,)) for k in every]
    return out


def shards(tokens, weights, key_mask, w_query, w_key, w_value, w_out):
    rows, cells, width = tokens.shape
    inner = w_query.shape[1]
    tiles = inner // LANES
    blocks = lax.axis_size("res")
    holders = lax.axis_size("seq")
    cores = lax.axis_size("head")
    part = HEAD_DIM
    share = rows // cores
    assert share * cores == rows and tiles * LANES == inner and part * CHUNKS == cells == LANES
    f32, bf16 = jnp.float32, jnp.bfloat16
    masked = MASKED / holders
    shape = pltpu.VMEM
    key_mask = key_mask.reshape(1, cells)

    length = share * part * width // LANES
    hbm = pl.BlockSpec(memory_space=pltpu.HBM)
    moving = [
        pl.pallas_call(
            functools.partial(pack_kernel, chunk=k, share=share),
            out_shape=shape((length + (0 if k else MARK_ROWS), LANES), bf16),
            in_specs=[hbm, hbm],
            out_specs=whole(1)[0],
            scratch_shapes=[
                shape((share, part, width), bf16),
                shape((1, cells), jnp.int32),
                pltpu.SemaphoreType.DMA((2,)),
            ],
            compiler_params=pltpu.CompilerParams(vmem_limit_bytes=VMEM_LIMIT),
        )(pltpu.with_memory_space_constraint(tokens, pltpu.HBM), pltpu.with_memory_space_constraint(key_mask, pltpu.HBM))
        for k in range(CHUNKS)
    ]
    counts = [weights]
    for k in range(1, holders):
        counts.append(ring(weights, "seq", k))

    def exchange(logits):
        return [logits] + [ring(logits, "seq", k) for k in range(1, holders)]

    depth = PER_TILE * part
    spans = rows * LANES
    query, logits, values = call(
        functools.partial(own_kernel, cores=cores, masked=masked),
        [
            shape((tiles, cells, spans), bf16),
            shape((CHUNKS, tiles, cells, depth), f32),
            shape((CHUNKS, tiles, depth, spans), bf16),
        ],
        counts + [key_mask, tokens, w_query, w_key, w_value],
        2 * rows * cells * inner * (3 * width + cells * PER_TILE),
        holders,
        [pltpu.VMEM((CHUNKS, tiles, depth, spans), bf16)],
    )
    units = [(exchange(logits), values)]

    pieces, moved = {}, {}
    for step in range(1, blocks):
        moving = [ring(moving[k], "res") for k in range(CHUNKS)]
        moved[step] = moving[0]
        for k in range(CHUNKS):
            pieces[step, k] = [moving[k]] + [ring(moving[k], "head", j) for j in range(1, cores)]

    def kernel(function, outs, args, rows, both, scratch_rows):
        return call(
            function,
            outs,
            args,
            2 * rows * part * inner * (both * width + cells * PER_TILE),
            0,
            [shape((1, tiles, depth, scratch_rows * LANES), bf16)] if scratch_rows else (),
        )

    for step, taken in batches(blocks):
        count = len(taken)
        logits_shape = shape((count, tiles, cells, depth), f32)
        values_shape = shape((count, tiles, depth, spans), bf16)
        if count > 1 or cores == 1:
            mine = sum([pieces[step, k] for k in taken], [])
            project = functools.partial(project_kernel, order=taken, masked=masked)
            logits, values = kernel(
                project,
                [logits_shape, values_shape],
                [query, w_key, w_value] + mine,
                rows * count,
                2,
                rows,
            )
            units.append((exchange(logits), values))
            continue
        mine, marks = pieces[step, taken[0]], moved[step]
        early = kernel(early_kernel, logits_shape, [query, w_key, mine[0]], share, 1, share)
        late = functools.partial(late_kernel, chunk=taken[0], masked=masked)
        logits = kernel(
            late,
            logits_shape,
            [query, w_key, marks, early] + mine[1:],
            rows - share,
            1,
            rows - share,
        )
        shared = exchange(logits)
        values = kernel(values_kernel, values_shape, [w_value] + mine, rows, 1, 0)
        units.append((shared, values))

    state = []
    state_shape = [
        shape((tiles, cells, LANES), f32),
        shape((tiles, cells, LANES), f32),
        shape((tiles, cells, spans), f32),
    ]

    def flatten(group):
        return sum([list(u[0]) + [u[1]] for u in group], [])

    def work(group):
        return sum(2 * u[0][0].size * spans for u in group)

    cuts = groups_of(len(units))
    for cut in cuts[:-1]:
        group = units[slice(*cut)]
        state = call(
            functools.partial(absorb_kernel, sizes=[len(u[0]) for u in group], carried=bool(state)),
            state_shape,
            flatten(group) + list(state),
            work(group),
        )
    group = units[slice(*cuts[-1])]
    columns = width // cores
    attended, sent = call(
        functools.partial(
            finish_kernel, sizes=[len(u[0]) for u in group], carried=bool(state), cores=cores
        ),
        [shape((rows, cells, inner), bf16), shape((rows, cells, columns), bf16)],
        flatten(group) + list(state) + [w_out],
        work(group) + 2 * rows * cells * inner * columns,
    )

    def output(k):
        return call(
            functools.partial(output_kernel, ahead=k, cores=cores),
            shape((rows, cells, columns), f32),
            [attended, w_out],
            2 * rows * cells * inner * columns,
        )

    if cores == 1:
        return sent
    received = [ring(sent, "head")]
    for k in range(2, cores):
        received.append(ring(output(k).astype(bf16), "head", k))
    result = output(0)
    for value in received:
        result = result + value.astype(f32)
    return result.astype(bf16)


def groups_of(count):
    return [(at, min(at + 3, count - 1)) for at in range(0, count - 1, 3)] + [(count - 1, count)]


def solution(mesh):
    in_specs = (
        P(("grp", "seq"), "res", None),
        P(("grp", "seq")),
        P(("grp", "res")),
        P(None, "head"),
        P(None, "head"),
        P(None, "head"),
        P("head", None),
    )
    out_specs = P(("grp", "seq"), "res", "head")

    return jax.shard_map(shards, mesh=mesh, in_specs=in_specs, out_specs=out_specs, check_vma=False)
```

```python
import functools
import math

import jax
import jax.numpy as jnp
from jax import lax
from jax.experimental import pallas as pl
from jax.experimental.pallas import tpu as pltpu
from jax.sharding import PartitionSpec as P


HEAD_DIM = 64
LANES = 128
PER_TILE = LANES // HEAD_DIM
CHUNKS = 2
MARK_ROWS = 8
PIECE = 32
PARTS = HEAD_DIM // PIECE
MASKED = -1000000000.0
VMEM_LIMIT = 24 * 1024 * 1024


def ring(value, axis, by=1):
    length = lax.axis_size(axis)
    return lax.ppermute(value, axis, [(i, (i + by) % length) for i in range(length)])


def whole(count):
    return [pl.BlockSpec(memory_space=pltpu.VMEM) for _ in range(count)]


def call(kernel, out_shape, args, flops, scalars=0, scratch=()):
    specs = [pl.BlockSpec(memory_space=pltpu.SMEM)] * scalars + whole(len(args) - scalars)
    multiple = isinstance(out_shape, (list, tuple))
    size = sum(a.size * a.dtype.itemsize for a in args)
    return pl.pallas_call(
        kernel,
        out_shape=out_shape,
        in_specs=specs,
        out_specs=whole(len(out_shape)) if multiple else whole(1)[0],
        scratch_shapes=list(scratch),
        cost_estimate=pl.CostEstimate(flops=int(flops), transcendentals=0, bytes_accessed=int(size)),
        compiler_params=pltpu.CompilerParams(vmem_limit_bytes=VMEM_LIMIT),
    )(*args)


def lane_head(shape):
    return lax.broadcasted_iota(jnp.int32, shape, len(shape) - 1) // HEAD_DIM


def dot(a, b):
    return jnp.dot(a, b, preferred_element_type=jnp.float32)


def dot_nt(a, b):
    return lax.dot_general(a, b, (((1,), (1,)), ((), ())), preferred_element_type=jnp.float32)


def per_head(value, pick):
    heads = lane_head(value.shape)
    parts = [pick(value, heads == h) for h in range(PER_TILE)]
    out = parts[-1]
    for h in range(PER_TILE - 2, -1, -1):
        out = jnp.where(heads == h, parts[h], out)
    return jnp.broadcast_to(out, value.shape)


def max_over(value, keep):
    return jnp.max(jnp.where(keep, value, -jnp.inf), axis=-1, keepdims=True)


def sum_over(value, keep):
    return jnp.sum(jnp.where(keep, value, 0.0), axis=-1, keepdims=True)


def spread(target, chunk, flat, first_row, cells):
    rows = flat.shape[0] // cells
    tiles = flat.shape[1] // LANES
    heads = lane_head((cells, LANES))
    for tile in range(tiles):
        for row in range(rows):
            part = flat[row * cells : (row + 1) * cells, tile * LANES : (tile + 1) * LANES]
            at = slice((first_row + row) * LANES, (first_row + row + 1) * LANES)
            for h in range(PER_TILE):
                kept = jnp.where(heads == h, part, jnp.zeros_like(part))
                target[chunk, tile, h * cells : (h + 1) * cells, at] = kept


def own_row(row, share, cores):
    core = lax.axis_index("head")
    return lax.rem(core + (cores - row // share), cores) * share + row % share


def live_lanes(mask, chunk):
    turned = pltpu.roll(mask, HEAD_DIM, 1)
    first = lane_head(mask.shape) == 0
    return (jnp.where(first, mask, turned) if chunk == 0 else jnp.where(first, turned, mask))[:1] > 0


def score(query, keys, live, masked):
    return jnp.where(live, dot_nt(query, keys), masked)


def pack_kernel(tokens, mask, packed, landing, marks, done, *, chunk, share):
    _, part, width = landing.shape
    core = lax.axis_index("head")
    size = share * part
    used = width // LANES * size
    copies = [
        pltpu.make_async_copy(
            tokens.at[pl.ds(core * share, share), pl.ds(chunk * part, part)], landing, done.at[0]
        )
    ]
    if packed.shape[0] > used:
        copies.append(pltpu.make_async_copy(mask, marks, done.at[1]))
    for copy in copies:
        copy.start()
    for copy in copies:
        copy.wait()
    for tile in range(width // LANES):
        at = slice(tile * LANES, (tile + 1) * LANES)
        packed[tile * size : (tile + 1) * size] = landing[:, :, at].reshape(size, LANES)
    if packed.shape[0] > used:
        tail = packed.shape[0] - used
        packed[used:] = jnp.broadcast_to(marks[...].astype(jnp.float32), (tail, LANES)).astype(jnp.bfloat16)


def unpack(pieces, width):
    tiles = width // LANES
    flats = []
    for piece in pieces:
        size = piece.shape[0] // tiles // PIECE * PIECE
        flats.append(
            jnp.concatenate([piece[tile * size : (tile + 1) * size] for tile in range(tiles)], axis=1)
        )
    return jnp.concatenate(flats, axis=0)


def marks_of(piece):
    return piece[piece.shape[0] - MARK_ROWS :].astype(jnp.float32)


def project_kernel(*refs, order, masked):
    query, w_key, w_value = refs[:3]
    pieces = refs[3:-3]
    logits, values, keys = refs[-3:]
    width = w_key.shape[0]
    per_chunk = len(pieces) // len(order)
    part = keys.shape[2] // PER_TILE
    for at, chunk in enumerate(order):
        flat = unpack(pieces[at * per_chunk : (at + 1) * per_chunk], width)
        spread(keys, 0, dot(flat, w_key[...]).astype(jnp.bfloat16), 0, part)
        live = live_lanes(marks_of(pieces[0]), chunk)
        for tile in range(query.shape[0]):
            logits[at, tile] = score(query[tile], keys[0, tile], live, masked)
        spread(values, at, dot(flat, w_value[...]).astype(jnp.bfloat16), 0, part)


def early_kernel(query, w_key, piece, logits, keys):
    spread(keys, 0, dot(unpack([piece], w_key.shape[0]), w_key[...]).astype(jnp.bfloat16), 0, HEAD_DIM)
    for tile in range(query.shape[0]):
        logits[0, tile] = dot_nt(query[tile, :, : keys.shape[3]], keys[0, tile])


def late_kernel(query, w_key, marks, before, *refs, chunk, masked):
    pieces, (logits, keys) = refs[:-2], refs[-2:]
    flat = unpack(pieces, w_key.shape[0])
    spread(keys, 0, dot(flat, w_key[...]).astype(jnp.bfloat16), 0, HEAD_DIM)
    live = live_lanes(marks_of(marks), chunk)
    skip = query.shape[2] - keys.shape[3]
    for tile in range(query.shape[0]):
        total = before[0, tile] + dot_nt(query[tile, :, skip:], keys[0, tile])
        logits[0, tile] = jnp.where(live, total, masked)


def values_kernel(w_value, *refs):
    pieces, values = refs[:-1], refs[-1]
    flat = unpack(pieces, w_value.shape[0])
    spread(values, 0, dot(flat, w_value[...]).astype(jnp.bfloat16), 0, HEAD_DIM)


def split_kernel(packed, *parts, tiles):
    size = packed.shape[0] // tiles // PIECE * PIECE
    count = len(parts)
    for at, part in enumerate(parts):
        for block in range(tiles * size // PIECE // count):
            source = (block * count + at) * PIECE
            part[block * PIECE : (block + 1) * PIECE] = packed[source : source + PIECE]
    if packed.shape[0] > tiles * size:
        parts[0][tiles * size // count :] = packed[tiles * size :]


def tall_early_kernel(query, w_key, piece, logits, keys):
    spread(keys, 0, dot(unpack([piece], w_key.shape[0]), w_key[...]).astype(jnp.bfloat16), 0, PIECE)
    for tile in range(query.shape[0]):
        logits[tile] = dot_nt(keys[0, tile], query[tile, :, : keys.shape[3]])


def tall_late_kernel(query, w_key, marks, before, *refs, first, masked):
    pieces, (logits, keys) = refs[:-2], refs[-2:]
    flat = unpack(pieces, w_key.shape[0])
    spread(keys, 0, dot(flat, w_key[...]).astype(jnp.bfloat16), 0, PIECE)
    grid = logits.shape[1:]
    cell = lax.broadcasted_iota(jnp.int32, grid, 0) % PIECE + first
    here = cell == lax.broadcasted_iota(jnp.int32, grid, 1)
    mask = jnp.broadcast_to(marks_of(marks)[:1], grid)
    live = jnp.max(jnp.where(here, mask, 0.0), axis=1, keepdims=True) > 0
    skip = query.shape[2] - keys.shape[3]
    for tile in range(query.shape[0]):
        total = before[tile] + dot_nt(keys[0, tile], query[tile, :, skip:])
        logits[tile] = jnp.where(live, total, masked)


def tall_values_kernel(w_value, *refs):
    pieces, values = refs[:-1], refs[-1]
    per_piece = len(pieces) // PARTS
    for at in range(PARTS):
        flat = unpack(pieces[at * per_piece : (at + 1) * per_piece], w_value.shape[0])
        flat = dot(flat, w_value[...]).astype(jnp.bfloat16)
        rows = flat.shape[0] // PIECE
        heads = lane_head((PIECE, LANES))
        for tile in range(flat.shape[1] // LANES):
            for row in range(rows):
                part = flat[row * PIECE : (row + 1) * PIECE, tile * LANES : (tile + 1) * LANES]
                for h in range(PER_TILE):
                    kept = jnp.where(heads == h, part, jnp.zeros_like(part))
                    top = h * HEAD_DIM + at * PIECE
                    values[0, tile, top : top + PIECE, row * LANES : (row + 1) * LANES] = kept


def upright(parts):
    rows = [part[h * PIECE : (h + 1) * PIECE] for h in range(PER_TILE) for part in parts]
    return jnp.concatenate(rows, axis=0).T


def own_kernel(*refs, cores, masked):
    counts, refs = refs[:-9], refs[-9:]
    mask, tokens, w_query, w_key, w_value, query, logits, values, keys = refs
    rows, cells, _ = tokens.shape
    chunks = logits.shape[0]
    part = cells // chunks
    total = sum(count[row] for count in counts for row in range(rows))
    scale = lax.rsqrt(jnp.full((1, query.shape[0] * LANES), total, jnp.int32).astype(jnp.float32))
    for row in range(rows):
        source = own_row(row, rows // cores, cores)
        block = tokens[source]
        count = jnp.full(scale.shape, counts[0][source], jnp.int32).astype(jnp.float32)
        factor = count * scale / math.sqrt(HEAD_DIM)
        scaled = (dot(block, w_query[...]) * factor).astype(jnp.bfloat16)
        for tile in range(query.shape[0]):
            query[tile, :, row * LANES : (row + 1) * LANES] = scaled[:, tile * LANES : (tile + 1) * LANES]
        key = dot(block, w_key[...]).astype(jnp.bfloat16)
        value = dot(block, w_value[...]).astype(jnp.bfloat16)
        for chunk in range(chunks):
            spread(keys, chunk, key[chunk * part : (chunk + 1) * part], row, part)
            spread(values, chunk, value[chunk * part : (chunk + 1) * part], row, part)
    marks = jnp.broadcast_to(mask[...].astype(jnp.float32), (8, LANES))
    for chunk in range(chunks):
        live = live_lanes(marks, chunk)
        for tile in range(query.shape[0]):
            logits[chunk, tile] = score(query[tile], keys[chunk, tile], live, masked)


def absorb(units, state, tile, rows):
    scores, mixed = [], []
    for pieces, values in units:
        whole_chunks = len(pieces) == 1
        for chunk in range(values.shape[0]):
            totals = []
            for tiles in pieces:
                total = tiles[0][chunk, tile] if whole_chunks else tiles[0][tile]
                for other in tiles[1:]:
                    total = total + (other[chunk, tile] if whole_chunks else other[tile])
                totals.append(total)
            scores.append(totals[0] if whole_chunks else upright(totals))
            mixed.append(values[chunk, tile])
    top = functools.reduce(jnp.maximum, scores)
    top = per_head(top, max_over)
    if state is not None:
        before = state[0][tile]
        top = jnp.maximum(top, before)
        rescale = jnp.exp(before - top)
    expo = [jnp.exp(score - top) for score in scores]
    denom = functools.reduce(jnp.add, expo)
    probs = jnp.concatenate([e.astype(jnp.bfloat16) for e in expo], axis=1)
    accum = dot(probs, jnp.concatenate(mixed, axis=0))
    if state is not None:
        denom = denom + state[1][tile] * rescale
        accum = accum + state[2][tile] * jnp.concatenate([rescale] * rows, axis=1)
    return top, denom, accum


def read_units(refs, sizes):
    units, at = [], 0
    for parts, size in sizes:
        pieces = [refs[at + n * size : at + (n + 1) * size] for n in range(parts)]
        at += parts * size
        units.append((pieces, refs[at]))
        at += 1
    return units, refs[at:]


def absorb_kernel(*refs, sizes, carried):
    units, refs = read_units(refs, sizes)
    state = refs[:3] if carried else None
    top, denom, accum = refs[-3:]
    rows = accum.shape[2] // LANES
    for tile in range(accum.shape[0]):
        top[tile], denom[tile], accum[tile] = absorb(units, state, tile, rows)


def columns_of(w_out, ahead, cores):
    columns = w_out.shape[1] // cores
    at = lax.rem(lax.axis_index("head") + ahead, cores) * columns
    return w_out[:, pl.ds(pl.multiple_of(at, LANES), columns)]


def finish_kernel(*refs, sizes, carried, cores):
    units, refs = read_units(refs, sizes)
    state = refs[:3] if carried else None
    w_out, attended, sent = refs[-3:]
    rows, _, _ = attended.shape
    for tile in range(attended.shape[2] // LANES):
        _, denom, accum = absorb(units, state, tile, rows)
        denom = per_head(denom, sum_over)
        for row in range(rows):
            part = accum[:, row * LANES : (row + 1) * LANES] / denom
            attended[row, :, tile * LANES : (tile + 1) * LANES] = part.astype(jnp.bfloat16)
    write_output(attended, columns_of(w_out, 1 % cores, cores), sent, cores)


def write_output(attended, w, target, cores):
    rows = attended.shape[0]
    for row in range(rows):
        target[own_row(row, rows // cores, cores)] = dot(attended[row], w).astype(target.dtype)


def output_kernel(attended, w_out, kept, *, ahead, cores):
    write_output(attended, columns_of(w_out, ahead, cores), kept, cores)


def batches(blocks):
    every = tuple(range(CHUNKS))
    out = []
    for step in range(1, blocks - 1):
        if step < blocks - 2:
            out.append((step, every))
        else:
            out += [(step, (k,)) for k in every]
    return out


def shards(tokens, weights, key_mask, w_query, w_key, w_value, w_out):
    rows, cells, width = tokens.shape
    inner = w_query.shape[1]
    tiles = inner // LANES
    blocks = lax.axis_size("res")
    holders = lax.axis_size("seq")
    cores = lax.axis_size("head")
    part = HEAD_DIM
    share = rows // cores
    assert share * cores == rows and tiles * LANES == inner and part * CHUNKS == cells == LANES
    f32, bf16 = jnp.float32, jnp.bfloat16
    masked = MASKED / holders
    shape = pltpu.VMEM
    key_mask = key_mask.reshape(1, cells)

    length = share * part * width // LANES
    hbm = pl.BlockSpec(memory_space=pltpu.HBM)
    moving = [
        pl.pallas_call(
            functools.partial(pack_kernel, chunk=k, share=share),
            out_shape=shape((length + (0 if k else MARK_ROWS), LANES), bf16),
            in_specs=[hbm, hbm],
            out_specs=whole(1)[0],
            scratch_shapes=[
                shape((share, part, width), bf16),
                shape((1, cells), jnp.int32),
                pltpu.SemaphoreType.DMA((2,)),
            ],
            compiler_params=pltpu.CompilerParams(vmem_limit_bytes=VMEM_LIMIT),
        )(pltpu.with_memory_space_constraint(tokens, pltpu.HBM), pltpu.with_memory_space_constraint(key_mask, pltpu.HBM))
        for k in range(CHUNKS)
    ]
    counts = [weights]
    for k in range(1, holders):
        counts.append(ring(weights, "seq", k))

    def exchange(logits):
        return [logits] + [ring(logits, "seq", k) for k in range(1, holders)]

    depth = PER_TILE * part
    spans = rows * LANES
    query, logits, values = call(
        functools.partial(own_kernel, cores=cores, masked=masked),
        [
            shape((tiles, cells, spans), bf16),
            shape((CHUNKS, tiles, cells, depth), f32),
            shape((CHUNKS, tiles, depth, spans), bf16),
        ],
        counts + [key_mask, tokens, w_query, w_key, w_value],
        2 * rows * cells * inner * (3 * width + cells * PER_TILE),
        holders,
        [pltpu.VMEM((CHUNKS, tiles, depth, spans), bf16)],
    )
    units = [([exchange(logits)], values)]

    pieces, moved = {}, {}

    def shared_rows(value):
        return [value] + [ring(value, "head", j) for j in range(1, cores)]

    fine = []
    for step in range(1, blocks):
        if step == blocks - 1:
            for k in range(CHUNKS):
                size = moving[k].shape[0] // (PARTS * PIECE) * PIECE
                rest = moving[k].shape[0] - PARTS * size
                cut = call(
                    functools.partial(split_kernel, tiles=width // LANES),
                    [shape((size + (0 if n else rest), LANES), bf16) for n in range(PARTS)],
                    [moving[k]],
                    0,
                )
                fine += cut
            fine = [ring(fine[q], "res") for q in range(len(fine))]
            break
        moving = [ring(moving[k], "res") for k in range(CHUNKS)]
        moved[step] = moving[0]
        for k in range(CHUNKS):
            pieces[step, k] = shared_rows(moving[k])

    def kernel(function, outs, args, rows, both, scratch_rows, high=part):
        return call(
            function,
            outs,
            args,
            2 * rows * part * inner * (both * width + cells * PER_TILE),
            0,
            [shape((1, tiles, PER_TILE * high, scratch_rows * LANES), bf16)] if scratch_rows else (),
        )

    for step, taken in batches(blocks):
        count = len(taken)
        logits_shape = shape((count, tiles, cells, depth), f32)
        values_shape = shape((count, tiles, depth, spans), bf16)
        if count > 1 or cores == 1:
            mine = sum([pieces[step, k] for k in taken], [])
            project = functools.partial(project_kernel, order=taken, masked=masked)
            logits, values = kernel(
                project, [logits_shape, values_shape], [query, w_key, w_value] + mine, rows * count, 2, rows
            )
            units.append(([exchange(logits)], values))
            continue
        mine, marks = pieces[step, taken[0]], moved[step]
        early = kernel(early_kernel, logits_shape, [query, w_key, mine[0]], share, 1, share)
        late = functools.partial(late_kernel, chunk=taken[0], masked=masked)
        logits = kernel(late, logits_shape, [query, w_key, marks, early] + mine[1:], rows - share, 1, rows - share)
        shared = exchange(logits)
        values = kernel(values_kernel, values_shape, [w_value] + mine, rows, 1, 0)
        units.append(([shared], values))

    tall = []
    for q, piece in enumerate(fine):
        logits_shape = shape((tiles, PER_TILE * PIECE, cells), f32)
        mine = shared_rows(piece)
        early = kernel(tall_early_kernel, logits_shape, [query, w_key, piece], share / 2, 1, share, PIECE)
        late = functools.partial(tall_late_kernel, first=q * PIECE, masked=masked)
        logits = kernel(
            late, logits_shape, [query, w_key, fine[0], early] + mine[1:], (rows - share) / 2, 1, rows - share, PIECE
        )
        tall.append((exchange(logits), mine))
    for k in range(len(tall) // PARTS):
        group = tall[k * PARTS : (k + 1) * PARTS]
        values = kernel(
            tall_values_kernel,
            shape((1, tiles, depth, spans), bf16),
            [w_value] + sum([mine for _, mine in group], []),
            rows,
            1,
            0,
        )
        units.append(([shared for shared, _ in group], values))

    state = []
    state_shape = [
        shape((tiles, cells, LANES), f32),
        shape((tiles, cells, LANES), f32),
        shape((tiles, cells, spans), f32),
    ]

    def flatten(group):
        return sum([sum([list(piece) for piece in u[0]], []) + [u[1]] for u in group], [])

    def work(group):
        return sum(2 * cells * u[1].size for u in group)

    def sizes_of(group):
        return [(len(u[0]), len(u[0][0])) for u in group]

    cuts = groups_of(len(units))
    for cut in cuts[:-1]:
        group = units[slice(*cut)]
        state = call(
            functools.partial(absorb_kernel, sizes=sizes_of(group), carried=bool(state)),
            state_shape,
            flatten(group) + list(state),
            work(group),
        )
    group = units[slice(*cuts[-1])]
    columns = width // cores
    attended, sent = call(
        functools.partial(
            finish_kernel, sizes=sizes_of(group), carried=bool(state), cores=cores
        ),
        [shape((rows, cells, inner), bf16), shape((rows, cells, columns), bf16)],
        flatten(group) + list(state) + [w_out],
        work(group) + 2 * rows * cells * inner * columns,
    )

    def output(k):
        return call(
            functools.partial(output_kernel, ahead=k, cores=cores),
            shape((rows, cells, columns), f32),
            [attended, w_out],
            2 * rows * cells * inner * columns,
        )

    if cores == 1:
        return sent
    received = [ring(sent, "head")]
    for k in range(2, cores):
        received.append(ring(output(k).astype(bf16), "head", k))
    result = output(0)
    for value in received:
        result = result + value.astype(f32)
    return result.astype(bf16)


def groups_of(count):
    return [(at, min(at + 3, count - 1)) for at in range(0, count - 1, 3)] + [(count - 1, count)]


def solution(mesh):
    in_specs = (
        P(("grp", "seq"), "res", None),
        P(("grp", "seq")),
        P(("grp", "res")),
        P(None, "head"),
        P(None, "head"),
        P(None, "head"),
        P("head", None),
    )
    out_specs = P(("grp", "seq"), "res", "head")

    return jax.shard_map(shards, mesh=mesh, in_specs=in_specs, out_specs=out_specs, check_vma=False)
```

```python
import functools
import math

import jax
import jax.numpy as jnp
from jax import lax
from jax.experimental import pallas as pl
from jax.experimental.pallas import tpu as pltpu
from jax.sharding import PartitionSpec as P


HEAD_DIM = 64
LANES = 128
PER_TILE = LANES // HEAD_DIM
CHUNKS = 2
MARK_ROWS = 8
PIECE = 32
PARTS = HEAD_DIM // PIECE
MASKED = -1000000000.0
VMEM_LIMIT = 24 * 1024 * 1024


def ring(value, axis, by=1):
    length = lax.axis_size(axis)
    return lax.ppermute(value, axis, [(i, (i + by) % length) for i in range(length)])


def whole(count):
    return [pl.BlockSpec(memory_space=pltpu.VMEM) for _ in range(count)]


def call(kernel, out_shape, args, flops, scalars=0, scratch=()):
    specs = [pl.BlockSpec(memory_space=pltpu.SMEM)] * scalars + whole(len(args) - scalars)
    multiple = isinstance(out_shape, (list, tuple))
    size = sum(a.size * a.dtype.itemsize for a in args)
    return pl.pallas_call(
        kernel,
        out_shape=out_shape,
        in_specs=specs,
        out_specs=whole(len(out_shape)) if multiple else whole(1)[0],
        scratch_shapes=list(scratch),
        cost_estimate=pl.CostEstimate(flops=int(flops), transcendentals=0, bytes_accessed=int(size)),
        compiler_params=pltpu.CompilerParams(vmem_limit_bytes=VMEM_LIMIT),
    )(*args)


def lane_head(shape):
    return lax.broadcasted_iota(jnp.int32, shape, len(shape) - 1) // HEAD_DIM


def dot(a, b):
    return jnp.dot(a, b, preferred_element_type=jnp.float32)


def dot_nt(a, b):
    return lax.dot_general(a, b, (((1,), (1,)), ((), ())), preferred_element_type=jnp.float32)


def per_head(value, pick):
    heads = lane_head(value.shape)
    parts = [pick(value, heads == h) for h in range(PER_TILE)]
    out = parts[-1]
    for h in range(PER_TILE - 2, -1, -1):
        out = jnp.where(heads == h, parts[h], out)
    return jnp.broadcast_to(out, value.shape)


def max_over(value, keep):
    return jnp.max(jnp.where(keep, value, -jnp.inf), axis=-1, keepdims=True)


def sum_over(value, keep):
    return jnp.sum(jnp.where(keep, value, 0.0), axis=-1, keepdims=True)


def spread(target, chunk, flat, first_row, cells):
    rows = flat.shape[0] // cells
    tiles = flat.shape[1] // LANES
    heads = lane_head((cells, LANES))
    for tile in range(tiles):
        for row in range(rows):
            part = flat[row * cells : (row + 1) * cells, tile * LANES : (tile + 1) * LANES]
            at = slice((first_row + row) * LANES, (first_row + row + 1) * LANES)
            for h in range(PER_TILE):
                kept = jnp.where(heads == h, part, jnp.zeros_like(part))
                target[chunk, tile, h * cells : (h + 1) * cells, at] = kept


def own_row(row, share, cores):
    core = lax.axis_index("head")
    return lax.rem(core + (cores - row // share), cores) * share + row % share


def live_lanes(mask, chunk):
    turned = pltpu.roll(mask, HEAD_DIM, 1)
    first = lane_head(mask.shape) == 0
    return (jnp.where(first, mask, turned) if chunk == 0 else jnp.where(first, turned, mask))[:1] > 0


def score(query, keys, live, masked):
    return jnp.where(live, dot_nt(query, keys), masked)


def pack_kernel(tokens, mask, packed, landing, marks, done, *, chunk, share):
    _, part, width = landing.shape
    core = lax.axis_index("head")
    size = share * part
    used = width // LANES * size
    copies = [
        pltpu.make_async_copy(
            tokens.at[pl.ds(core * share, share), pl.ds(chunk * part, part)], landing, done.at[0]
        )
    ]
    if packed.shape[0] > used:
        copies.append(pltpu.make_async_copy(mask, marks, done.at[1]))
    for copy in copies:
        copy.start()
    for copy in copies:
        copy.wait()
    for tile in range(width // LANES):
        at = slice(tile * LANES, (tile + 1) * LANES)
        packed[tile * size : (tile + 1) * size] = landing[:, :, at].reshape(size, LANES)
    if packed.shape[0] > used:
        tail = packed.shape[0] - used
        packed[used:] = jnp.broadcast_to(marks[...].astype(jnp.float32), (tail, LANES)).astype(jnp.bfloat16)


def unpack(pieces, width):
    tiles = width // LANES
    flats = []
    for piece in pieces:
        size = piece.shape[0] // tiles // PIECE * PIECE
        flats.append(
            jnp.concatenate([piece[tile * size : (tile + 1) * size] for tile in range(tiles)], axis=1)
        )
    return jnp.concatenate(flats, axis=0)


def marks_of(piece):
    return piece[piece.shape[0] - MARK_ROWS :].astype(jnp.float32)


def project_kernel(*refs, order, masked):
    query, w_key, w_value = refs[:3]
    pieces = refs[3:-3]
    logits, values, keys = refs[-3:]
    width = w_key.shape[0]
    per_chunk = len(pieces) // len(order)
    part = keys.shape[2] // PER_TILE
    for at, chunk in enumerate(order):
        flat = unpack(pieces[at * per_chunk : (at + 1) * per_chunk], width)
        spread(keys, 0, dot(flat, w_key[...]).astype(jnp.bfloat16), 0, part)
        live = live_lanes(marks_of(pieces[0]), chunk)
        for tile in range(query.shape[0]):
            logits[at, tile] = score(query[tile], keys[0, tile], live, masked)
        spread(values, at, dot(flat, w_value[...]).astype(jnp.bfloat16), 0, part)


def early_kernel(query, w_key, piece, logits, keys):
    spread(keys, 0, dot(unpack([piece], w_key.shape[0]), w_key[...]).astype(jnp.bfloat16), 0, HEAD_DIM)
    for tile in range(query.shape[0]):
        logits[0, tile] = dot_nt(query[tile, :, : keys.shape[3]], keys[0, tile])


def late_kernel(query, w_key, marks, before, *refs, chunk, masked):
    pieces, (logits, keys) = refs[:-2], refs[-2:]
    flat = unpack(pieces, w_key.shape[0])
    spread(keys, 0, dot(flat, w_key[...]).astype(jnp.bfloat16), 0, HEAD_DIM)
    live = live_lanes(marks_of(marks), chunk)
    skip = query.shape[2] - keys.shape[3]
    for tile in range(query.shape[0]):
        total = before[0, tile] + dot_nt(query[tile, :, skip:], keys[0, tile])
        logits[0, tile] = jnp.where(live, total, masked)


def values_kernel(w_value, *refs):
    pieces, values = refs[:-1], refs[-1]
    flat = unpack(pieces, w_value.shape[0])
    spread(values, 0, dot(flat, w_value[...]).astype(jnp.bfloat16), 0, HEAD_DIM)


def split_kernel(packed, *parts, tiles):
    size = packed.shape[0] // tiles
    count = len(parts)
    for at, part in enumerate(parts):
        for block in range(tiles * size // PIECE // count):
            source = (block * count + at) * PIECE
            part[block * PIECE : (block + 1) * PIECE] = packed[source : source + PIECE]


def tall_early_kernel(query, w_key, piece, logits, keys):
    spread(keys, 0, dot(unpack([piece], w_key.shape[0]), w_key[...]).astype(jnp.bfloat16), 0, PIECE)
    for tile in range(query.shape[0]):
        logits[tile] = dot_nt(keys[0, tile], query[tile, :, : keys.shape[3]])


def tall_late_kernel(query, w_key, marks, before, *refs, first, masked):
    pieces, (logits, keys) = refs[:-2], refs[-2:]
    flat = unpack(pieces, w_key.shape[0])
    spread(keys, 0, dot(flat, w_key[...]).astype(jnp.bfloat16), 0, PIECE)
    grid = logits.shape[1:]
    cell = lax.broadcasted_iota(jnp.int32, grid, 0) % PIECE + first
    here = cell == lax.broadcasted_iota(jnp.int32, grid, 1)
    mask = jnp.broadcast_to(marks_of(marks)[:1], grid)
    live = jnp.max(jnp.where(here, mask, 0.0), axis=1, keepdims=True) > 0
    skip = query.shape[2] - keys.shape[3]
    for tile in range(query.shape[0]):
        total = before[tile] + dot_nt(keys[0, tile], query[tile, :, skip:])
        logits[tile] = jnp.where(live, total, masked)


def tall_values_kernel(w_value, *refs):
    pieces, values = refs[:-1], refs[-1]
    per_piece = len(pieces) // PARTS
    for at in range(PARTS):
        flat = unpack(pieces[at * per_piece : (at + 1) * per_piece], w_value.shape[0])
        flat = dot(flat, w_value[...]).astype(jnp.bfloat16)
        rows = flat.shape[0] // PIECE
        heads = lane_head((PIECE, LANES))
        for tile in range(flat.shape[1] // LANES):
            for row in range(rows):
                part = flat[row * PIECE : (row + 1) * PIECE, tile * LANES : (tile + 1) * LANES]
                for h in range(PER_TILE):
                    kept = jnp.where(heads == h, part, jnp.zeros_like(part))
                    top = h * HEAD_DIM + at * PIECE
                    values[0, tile, top : top + PIECE, row * LANES : (row + 1) * LANES] = kept


def upright(parts):
    rows = [part[h * PIECE : (h + 1) * PIECE] for h in range(PER_TILE) for part in parts]
    return jnp.concatenate(rows, axis=0).T


def own_kernel(*refs, cores, masked):
    counts, refs = refs[:-9], refs[-9:]
    mask, tokens, w_query, w_key, w_value, query, logits, values, keys = refs
    rows, cells, _ = tokens.shape
    chunks = logits.shape[0]
    part = cells // chunks
    total = sum(count[row] for count in counts for row in range(rows))
    scale = lax.rsqrt(jnp.full((1, query.shape[0] * LANES), total, jnp.int32).astype(jnp.float32))
    for row in range(rows):
        source = own_row(row, rows // cores, cores)
        block = tokens[source]
        count = jnp.full(scale.shape, counts[0][source], jnp.int32).astype(jnp.float32)
        factor = count * scale / math.sqrt(HEAD_DIM)
        scaled = (dot(block, w_query[...]) * factor).astype(jnp.bfloat16)
        for tile in range(query.shape[0]):
            query[tile, :, row * LANES : (row + 1) * LANES] = scaled[:, tile * LANES : (tile + 1) * LANES]
        key = dot(block, w_key[...]).astype(jnp.bfloat16)
        value = dot(block, w_value[...]).astype(jnp.bfloat16)
        for chunk in range(chunks):
            spread(keys, chunk, key[chunk * part : (chunk + 1) * part], row, part)
            spread(values, chunk, value[chunk * part : (chunk + 1) * part], row, part)
    marks = jnp.broadcast_to(mask[...].astype(jnp.float32), (8, LANES))
    for chunk in range(chunks):
        live = live_lanes(marks, chunk)
        for tile in range(query.shape[0]):
            logits[chunk, tile] = score(query[tile], keys[chunk, tile], live, masked)


def absorb(units, state, tile, rows):
    scores, mixed = [], []
    for pieces, values in units:
        whole_chunks = len(pieces) == 1
        for chunk in range(values.shape[0]):
            totals = []
            for tiles in pieces:
                total = tiles[0][chunk, tile] if whole_chunks else tiles[0][tile]
                for other in tiles[1:]:
                    total = total + (other[chunk, tile] if whole_chunks else other[tile])
                totals.append(total)
            scores.append(totals[0] if whole_chunks else upright(totals))
            mixed.append(values[chunk, tile])
    top = functools.reduce(jnp.maximum, scores)
    top = per_head(top, max_over)
    if state is not None:
        before = state[0][tile]
        top = jnp.maximum(top, before)
        rescale = jnp.exp(before - top)
    expo = [jnp.exp(score - top) for score in scores]
    denom = functools.reduce(jnp.add, expo)
    probs = jnp.concatenate([e.astype(jnp.bfloat16) for e in expo], axis=1)
    accum = dot(probs, jnp.concatenate(mixed, axis=0))
    if state is not None:
        denom = denom + state[1][tile] * rescale
        accum = accum + state[2][tile] * jnp.concatenate([rescale] * rows, axis=1)
    return top, denom, accum


def read_units(refs, sizes):
    units, at = [], 0
    for parts, size in sizes:
        pieces = [refs[at + n * size : at + (n + 1) * size] for n in range(parts)]
        at += parts * size
        units.append((pieces, refs[at]))
        at += 1
    return units, refs[at:]


def absorb_kernel(*refs, sizes, carried):
    units, refs = read_units(refs, sizes)
    state = refs[:3] if carried else None
    top, denom, accum = refs[-3:]
    rows = accum.shape[2] // LANES
    for tile in range(accum.shape[0]):
        top[tile], denom[tile], accum[tile] = absorb(units, state, tile, rows)


def columns_of(w_out, ahead, cores):
    columns = w_out.shape[1] // cores
    at = lax.rem(lax.axis_index("head") + ahead, cores) * columns
    return w_out[:, pl.ds(pl.multiple_of(at, LANES), columns)]


def finish_kernel(*refs, sizes, carried, cores):
    units, refs = read_units(refs, sizes)
    state = refs[:3] if carried else None
    w_out, attended, sent = refs[-3:]
    rows, _, _ = attended.shape
    for tile in range(attended.shape[2] // LANES):
        _, denom, accum = absorb(units, state, tile, rows)
        denom = per_head(denom, sum_over)
        for row in range(rows):
            part = accum[:, row * LANES : (row + 1) * LANES] / denom
            attended[row, :, tile * LANES : (tile + 1) * LANES] = part.astype(jnp.bfloat16)
    write_output(attended, columns_of(w_out, 1 % cores, cores), sent, cores)


def write_output(attended, w, target, cores):
    rows = attended.shape[0]
    for row in range(rows):
        target[own_row(row, rows // cores, cores)] = dot(attended[row], w).astype(target.dtype)


def output_kernel(attended, w_out, kept, *, ahead, cores):
    write_output(attended, columns_of(w_out, ahead, cores), kept, cores)


def batches(blocks):
    every = tuple(range(CHUNKS))
    out = []
    for step in range(1, blocks):
        if step < blocks - 2:
            out.append((step, every))
        else:
            out += [(step, (k,)) for k in every if (step, k) != (blocks - 1, CHUNKS - 1)]
    return out


def shards(tokens, weights, key_mask, w_query, w_key, w_value, w_out):
    rows, cells, width = tokens.shape
    inner = w_query.shape[1]
    tiles = inner // LANES
    blocks = lax.axis_size("res")
    holders = lax.axis_size("seq")
    cores = lax.axis_size("head")
    part = HEAD_DIM
    share = rows // cores
    assert share * cores == rows and tiles * LANES == inner and part * CHUNKS == cells == LANES
    f32, bf16 = jnp.float32, jnp.bfloat16
    masked = MASKED / holders
    shape = pltpu.VMEM
    key_mask = key_mask.reshape(1, cells)

    length = share * part * width // LANES
    hbm = pl.BlockSpec(memory_space=pltpu.HBM)
    moving = [
        pl.pallas_call(
            functools.partial(pack_kernel, chunk=k, share=share),
            out_shape=shape((length + (0 if k else MARK_ROWS), LANES), bf16),
            in_specs=[hbm, hbm],
            out_specs=whole(1)[0],
            scratch_shapes=[
                shape((share, part, width), bf16),
                shape((1, cells), jnp.int32),
                pltpu.SemaphoreType.DMA((2,)),
            ],
            compiler_params=pltpu.CompilerParams(vmem_limit_bytes=VMEM_LIMIT),
        )(pltpu.with_memory_space_constraint(tokens, pltpu.HBM), pltpu.with_memory_space_constraint(key_mask, pltpu.HBM))
        for k in range(CHUNKS)
    ]
    counts = [weights]
    for k in range(1, holders):
        counts.append(ring(weights, "seq", k))

    def exchange(logits):
        return [logits] + [ring(logits, "seq", k) for k in range(1, holders)]

    depth = PER_TILE * part
    spans = rows * LANES
    query, logits, values = call(
        functools.partial(own_kernel, cores=cores, masked=masked),
        [
            shape((tiles, cells, spans), bf16),
            shape((CHUNKS, tiles, cells, depth), f32),
            shape((CHUNKS, tiles, depth, spans), bf16),
        ],
        counts + [key_mask, tokens, w_query, w_key, w_value],
        2 * rows * cells * inner * (3 * width + cells * PER_TILE),
        holders,
        [pltpu.VMEM((CHUNKS, tiles, depth, spans), bf16)],
    )
    units = [([exchange(logits)], values)]

    pieces, moved = {}, {}

    def shared_rows(value):
        return [value] + [ring(value, "head", j) for j in range(1, cores)]

    last, tail = blocks - 1, CHUNKS - 1
    fine = []
    for step in range(1, blocks):
        if step == last:
            size = moving[tail].shape[0] // (PARTS * PIECE) * PIECE
            fine = call(
                functools.partial(split_kernel, tiles=width // LANES),
                [shape((size, LANES), bf16) for _ in range(PARTS)],
                [moving[tail]],
                0,
            )
            fine = [ring(fine[n], "res") for n in range(PARTS)]
        count = tail if step == last else CHUNKS
        moving = [ring(moving[k], "res") for k in range(count)]
        moved[step] = moving[0]
        for k in range(count):
            pieces[step, k] = shared_rows(moving[k])

    def kernel(function, outs, args, rows, both, scratch_rows, high=part):
        return call(
            function,
            outs,
            args,
            2 * rows * part * inner * (both * width + cells * PER_TILE),
            0,
            [shape((1, tiles, PER_TILE * high, scratch_rows * LANES), bf16)] if scratch_rows else (),
        )

    for step, taken in batches(blocks):
        count = len(taken)
        logits_shape = shape((count, tiles, cells, depth), f32)
        values_shape = shape((count, tiles, depth, spans), bf16)
        if count > 1 or cores == 1:
            mine = sum([pieces[step, k] for k in taken], [])
            project = functools.partial(project_kernel, order=taken, masked=masked)
            logits, values = kernel(
                project, [logits_shape, values_shape], [query, w_key, w_value] + mine, rows * count, 2, rows
            )
            units.append(([exchange(logits)], values))
            continue
        mine, marks = pieces[step, taken[0]], moved[step]
        early = kernel(early_kernel, logits_shape, [query, w_key, mine[0]], share, 1, share)
        late = functools.partial(late_kernel, chunk=taken[0], masked=masked)
        logits = kernel(late, logits_shape, [query, w_key, marks, early] + mine[1:], rows - share, 1, rows - share)
        shared = exchange(logits)
        values = kernel(values_kernel, values_shape, [w_value] + mine, rows, 1, 0)
        units.append(([shared], values))

    tall = []
    for n, piece in enumerate(fine):
        logits_shape = shape((tiles, PER_TILE * PIECE, cells), f32)
        mine = shared_rows(piece)
        early = kernel(tall_early_kernel, logits_shape, [query, w_key, piece], share / 2, 1, share, PIECE)
        late = functools.partial(tall_late_kernel, first=tail * part + n * PIECE, masked=masked)
        logits = kernel(
            late,
            logits_shape,
            [query, w_key, moved[last], early] + mine[1:],
            (rows - share) / 2,
            1,
            rows - share,
            PIECE,
        )
        tall.append((exchange(logits), mine))
    if tall:
        values = kernel(
            tall_values_kernel,
            shape((1, tiles, depth, spans), bf16),
            [w_value] + sum([mine for _, mine in tall], []),
            rows,
            1,
            0,
        )
        units.append(([shared for shared, _ in tall], values))

    state = []
    state_shape = [
        shape((tiles, cells, LANES), f32),
        shape((tiles, cells, LANES), f32),
        shape((tiles, cells, spans), f32),
    ]

    def flatten(group):
        return sum([sum([list(piece) for piece in u[0]], []) + [u[1]] for u in group], [])

    def work(group):
        return sum(2 * cells * u[1].size for u in group)

    def sizes_of(group):
        return [(len(u[0]), len(u[0][0])) for u in group]

    cuts = groups_of(len(units))
    for cut in cuts[:-1]:
        group = units[slice(*cut)]
        state = call(
            functools.partial(absorb_kernel, sizes=sizes_of(group), carried=bool(state)),
            state_shape,
            flatten(group) + list(state),
            work(group),
        )
    group = units[slice(*cuts[-1])]
    columns = width // cores
    attended, sent = call(
        functools.partial(
            finish_kernel, sizes=sizes_of(group), carried=bool(state), cores=cores
        ),
        [shape((rows, cells, inner), bf16), shape((rows, cells, columns), bf16)],
        flatten(group) + list(state) + [w_out],
        work(group) + 2 * rows * cells * inner * columns,
    )

    def output(k):
        return call(
            functools.partial(output_kernel, ahead=k, cores=cores),
            shape((rows, cells, columns), f32),
            [attended, w_out],
            2 * rows * cells * inner * columns,
        )

    if cores == 1:
        return sent
    received = [ring(sent, "head")]
    for k in range(2, cores):
        received.append(ring(output(k).astype(bf16), "head", k))
    result = output(0)
    for value in received:
        result = result + value.astype(f32)
    return result.astype(bf16)


def groups_of(count):
    return [(at, min(at + 3, count - 1)) for at in range(0, count - 1, 3)] + [(count - 1, count)]


def solution(mesh):
    in_specs = (
        P(("grp", "seq"), "res", None),
        P(("grp", "seq")),
        P(("grp", "res")),
        P(None, "head"),
        P(None, "head"),
        P(None, "head"),
        P("head", None),
    )
    out_specs = P(("grp", "seq"), "res", "head")

    return jax.shard_map(shards, mesh=mesh, in_specs=in_specs, out_specs=out_specs, check_vma=False)
```

```python
import functools
import math

import jax
import jax.numpy as jnp
from jax import lax
from jax.experimental import pallas as pl
from jax.experimental.pallas import tpu as pltpu
from jax.sharding import PartitionSpec as P


HEAD_DIM = 64
LANES = 128
PER_TILE = LANES // HEAD_DIM
CHUNKS = 2
MARK_ROWS = 8
PIECE = 32
PARTS = HEAD_DIM // PIECE
MASKED = -1000000000.0
VMEM_LIMIT = 24 * 1024 * 1024


def ring(value, axis, by=1):
    length = lax.axis_size(axis)
    return lax.ppermute(value, axis, [(i, (i + by) % length) for i in range(length)])


def whole(count):
    return [pl.BlockSpec(memory_space=pltpu.VMEM) for _ in range(count)]


def call(kernel, out_shape, args, flops, scalars=0, scratch=()):
    specs = [pl.BlockSpec(memory_space=pltpu.SMEM)] * scalars + whole(len(args) - scalars)
    multiple = isinstance(out_shape, (list, tuple))
    size = sum(a.size * a.dtype.itemsize for a in args)
    return pl.pallas_call(
        kernel,
        out_shape=out_shape,
        in_specs=specs,
        out_specs=whole(len(out_shape)) if multiple else whole(1)[0],
        scratch_shapes=list(scratch),
        cost_estimate=pl.CostEstimate(flops=int(flops), transcendentals=0, bytes_accessed=int(size)),
        compiler_params=pltpu.CompilerParams(vmem_limit_bytes=VMEM_LIMIT),
    )(*args)


def lane_head(shape):
    return lax.broadcasted_iota(jnp.int32, shape, len(shape) - 1) // HEAD_DIM


def dot(a, b):
    return jnp.dot(a, b, preferred_element_type=jnp.float32)


def dot_nt(a, b):
    return lax.dot_general(a, b, (((1,), (1,)), ((), ())), preferred_element_type=jnp.float32)


def per_head(value, pick):
    heads = lane_head(value.shape)
    parts = [pick(value, heads == h) for h in range(PER_TILE)]
    out = parts[-1]
    for h in range(PER_TILE - 2, -1, -1):
        out = jnp.where(heads == h, parts[h], out)
    return jnp.broadcast_to(out, value.shape)


def max_over(value, keep):
    return jnp.max(jnp.where(keep, value, -jnp.inf), axis=-1, keepdims=True)


def sum_over(value, keep):
    return jnp.sum(jnp.where(keep, value, 0.0), axis=-1, keepdims=True)


def spread(target, chunk, flat, first_row, cells):
    rows = flat.shape[0] // cells
    tiles = flat.shape[1] // LANES
    heads = lane_head((cells, LANES))
    for tile in range(tiles):
        for row in range(rows):
            part = flat[row * cells : (row + 1) * cells, tile * LANES : (tile + 1) * LANES]
            at = slice((first_row + row) * LANES, (first_row + row + 1) * LANES)
            for h in range(PER_TILE):
                kept = jnp.where(heads == h, part, jnp.zeros_like(part))
                target[chunk, tile, h * cells : (h + 1) * cells, at] = kept


def own_row(row, share, cores):
    core = lax.axis_index("head")
    return lax.rem(core + (cores - row // share), cores) * share + row % share


def live_lanes(mask, chunk):
    turned = pltpu.roll(mask, HEAD_DIM, 1)
    first = lane_head(mask.shape) == 0
    return (jnp.where(first, mask, turned) if chunk == 0 else jnp.where(first, turned, mask))[:1] > 0


def score(query, keys, live, masked):
    return jnp.where(live, dot_nt(query, keys), masked)


def pack_kernel(tokens, mask, packed, landing, marks, done, *, chunk, share):
    _, part, width = landing.shape
    core = lax.axis_index("head")
    size = share * part
    used = width // LANES * size
    copies = [
        pltpu.make_async_copy(
            tokens.at[pl.ds(core * share, share), pl.ds(chunk * part, part)], landing, done.at[0]
        )
    ]
    if packed.shape[0] > used:
        copies.append(pltpu.make_async_copy(mask, marks, done.at[1]))
    for copy in copies:
        copy.start()
    for copy in copies:
        copy.wait()
    for tile in range(width // LANES):
        at = slice(tile * LANES, (tile + 1) * LANES)
        packed[tile * size : (tile + 1) * size] = landing[:, :, at].reshape(size, LANES)
    if packed.shape[0] > used:
        tail = packed.shape[0] - used
        packed[used:] = jnp.broadcast_to(marks[...].astype(jnp.float32), (tail, LANES)).astype(jnp.bfloat16)


def unpack(pieces, width):
    tiles = width // LANES
    flats = []
    for piece in pieces:
        size = piece.shape[0] // tiles // PIECE * PIECE
        flats.append(
            jnp.concatenate([piece[tile * size : (tile + 1) * size] for tile in range(tiles)], axis=1)
        )
    return jnp.concatenate(flats, axis=0)


def marks_of(piece):
    return piece[piece.shape[0] - MARK_ROWS :].astype(jnp.float32)


def project_kernel(*refs, order, masked):
    query, w_key, w_value = refs[:3]
    pieces = refs[3:-3]
    logits, values, keys = refs[-3:]
    width = w_key.shape[0]
    per_chunk = len(pieces) // len(order)
    part = keys.shape[2] // PER_TILE
    for at, chunk in enumerate(order):
        flat = unpack(pieces[at * per_chunk : (at + 1) * per_chunk], width)
        spread(keys, 0, dot(flat, w_key[...]).astype(jnp.bfloat16), 0, part)
        live = live_lanes(marks_of(pieces[0]), chunk)
        for tile in range(query.shape[0]):
            logits[at, tile] = score(query[tile], keys[0, tile], live, masked)
        spread(values, at, dot(flat, w_value[...]).astype(jnp.bfloat16), 0, part)


def early_kernel(query, w_key, piece, logits, keys):
    spread(keys, 0, dot(unpack([piece], w_key.shape[0]), w_key[...]).astype(jnp.bfloat16), 0, HEAD_DIM)
    for tile in range(query.shape[0]):
        logits[0, tile] = dot_nt(query[tile, :, : keys.shape[3]], keys[0, tile])


def late_kernel(query, w_key, marks, before, *refs, chunk, masked):
    pieces, (logits, keys) = refs[:-2], refs[-2:]
    flat = unpack(pieces, w_key.shape[0])
    spread(keys, 0, dot(flat, w_key[...]).astype(jnp.bfloat16), 0, HEAD_DIM)
    live = live_lanes(marks_of(marks), chunk)
    skip = query.shape[2] - keys.shape[3]
    for tile in range(query.shape[0]):
        total = before[0, tile] + dot_nt(query[tile, :, skip:], keys[0, tile])
        logits[0, tile] = jnp.where(live, total, masked)


def values_kernel(w_value, *refs):
    pieces, values = refs[:-1], refs[-1]
    flat = unpack(pieces, w_value.shape[0])
    spread(values, 0, dot(flat, w_value[...]).astype(jnp.bfloat16), 0, HEAD_DIM)


def split_kernel(packed, *parts, tiles):
    size = packed.shape[0] // tiles
    count = len(parts)
    for at, part in enumerate(parts):
        for block in range(tiles * size // PIECE // count):
            source = (block * count + at) * PIECE
            part[block * PIECE : (block + 1) * PIECE] = packed[source : source + PIECE]


def tall_early_kernel(query, w_key, piece, logits, keys):
    spread(keys, 0, dot(unpack([piece], w_key.shape[0]), w_key[...]).astype(jnp.bfloat16), 0, PIECE)
    for tile in range(query.shape[0]):
        logits[tile] = dot_nt(keys[0, tile], query[tile, :, : keys.shape[3]])


def tall_late_kernel(query, w_key, marks, before, *refs, first, masked):
    pieces, (logits, keys) = refs[:-2], refs[-2:]
    flat = unpack(pieces, w_key.shape[0])
    spread(keys, 0, dot(flat, w_key[...]).astype(jnp.bfloat16), 0, PIECE)
    grid = logits.shape[1:]
    cell = lax.broadcasted_iota(jnp.int32, grid, 0) % PIECE + first
    here = cell == lax.broadcasted_iota(jnp.int32, grid, 1)
    mask = jnp.broadcast_to(marks_of(marks)[:1], grid)
    live = jnp.max(jnp.where(here, mask, 0.0), axis=1, keepdims=True) > 0
    skip = query.shape[2] - keys.shape[3]
    for tile in range(query.shape[0]):
        total = before[tile] + dot_nt(keys[0, tile], query[tile, :, skip:])
        logits[tile] = jnp.where(live, total, masked)


def tall_values_kernel(w_value, *refs):
    pieces, values = refs[:-1], refs[-1]
    per_piece = len(pieces) // PARTS
    for at in range(PARTS):
        flat = unpack(pieces[at * per_piece : (at + 1) * per_piece], w_value.shape[0])
        flat = dot(flat, w_value[...]).astype(jnp.bfloat16)
        rows = flat.shape[0] // PIECE
        heads = lane_head((PIECE, LANES))
        for tile in range(flat.shape[1] // LANES):
            for row in range(rows):
                part = flat[row * PIECE : (row + 1) * PIECE, tile * LANES : (tile + 1) * LANES]
                for h in range(PER_TILE):
                    kept = jnp.where(heads == h, part, jnp.zeros_like(part))
                    top = h * HEAD_DIM + at * PIECE
                    values[0, tile, top : top + PIECE, row * LANES : (row + 1) * LANES] = kept


def upright(parts):
    rows = [part[h * PIECE : (h + 1) * PIECE] for h in range(PER_TILE) for part in parts]
    return jnp.concatenate(rows, axis=0).T


def own_kernel(*refs, cores, masked):
    counts, refs = refs[:-9], refs[-9:]
    mask, tokens, w_query, w_key, w_value, query, logits, values, keys = refs
    rows, cells, _ = tokens.shape
    chunks = logits.shape[0]
    part = cells // chunks
    total = sum(count[row] for count in counts for row in range(rows))
    scale = lax.rsqrt(jnp.full((1, query.shape[0] * LANES), total, jnp.int32).astype(jnp.float32))
    for row in range(rows):
        source = own_row(row, rows // cores, cores)
        block = tokens[source]
        count = jnp.full(scale.shape, counts[0][source], jnp.int32).astype(jnp.float32)
        factor = count * scale / math.sqrt(HEAD_DIM)
        scaled = (dot(block, w_query[...]) * factor).astype(jnp.bfloat16)
        for tile in range(query.shape[0]):
            query[tile, :, row * LANES : (row + 1) * LANES] = scaled[:, tile * LANES : (tile + 1) * LANES]
        key = dot(block, w_key[...]).astype(jnp.bfloat16)
        value = dot(block, w_value[...]).astype(jnp.bfloat16)
        for chunk in range(chunks):
            spread(keys, chunk, key[chunk * part : (chunk + 1) * part], row, part)
            spread(values, chunk, value[chunk * part : (chunk + 1) * part], row, part)
    marks = jnp.broadcast_to(mask[...].astype(jnp.float32), (8, LANES))
    for chunk in range(chunks):
        live = live_lanes(marks, chunk)
        for tile in range(query.shape[0]):
            logits[chunk, tile] = score(query[tile], keys[chunk, tile], live, masked)


def absorb(units, state, tile, rows):
    scores, mixed = [], []
    for pieces, values in units:
        whole_chunks = len(pieces) == 1
        for chunk in range(values.shape[0]):
            totals = []
            for tiles in pieces:
                total = tiles[0][chunk, tile] if whole_chunks else tiles[0][tile]
                for other in tiles[1:]:
                    total = total + (other[chunk, tile] if whole_chunks else other[tile])
                totals.append(total)
            scores.append(totals[0] if whole_chunks else upright(totals))
            mixed.append(values[chunk, tile])
    top = functools.reduce(jnp.maximum, scores)
    top = per_head(top, max_over)
    if state is not None:
        before = state[0][tile]
        top = jnp.maximum(top, before)
        rescale = jnp.exp(before - top)
    expo = [jnp.exp(score - top) for score in scores]
    denom = functools.reduce(jnp.add, expo)
    probs = jnp.concatenate([e.astype(jnp.bfloat16) for e in expo], axis=1)
    accum = dot(probs, jnp.concatenate(mixed, axis=0))
    if state is not None:
        denom = denom + state[1][tile] * rescale
        accum = accum + state[2][tile] * jnp.concatenate([rescale] * rows, axis=1)
    return top, denom, accum


def read_units(refs, sizes):
    units, at = [], 0
    for parts, size in sizes:
        pieces = [refs[at + n * size : at + (n + 1) * size] for n in range(parts)]
        at += parts * size
        units.append((pieces, refs[at]))
        at += 1
    return units, refs[at:]


def absorb_kernel(*refs, sizes, carried):
    units, refs = read_units(refs, sizes)
    state = refs[:3] if carried else None
    top, denom, accum = refs[-3:]
    rows = accum.shape[2] // LANES
    for tile in range(accum.shape[0]):
        top[tile], denom[tile], accum[tile] = absorb(units, state, tile, rows)


def columns_kernel(w_out, *targets, cores):
    columns = w_out.shape[1] // cores
    for ahead, target in enumerate(targets):
        at = lax.rem(lax.axis_index("head") + ahead, cores) * columns
        target[...] = w_out[:, pl.ds(pl.multiple_of(at, LANES), columns)]


def finish_kernel(*refs, sizes, carried, cores, tile):
    units, refs = read_units(refs, sizes)
    state = refs[:3] if carried else None
    attended = refs[-1]
    rows = attended.shape[0]
    _, denom, accum = absorb(units, state, tile, rows)
    denom = per_head(denom, sum_over)
    for row in range(rows):
        part = accum[:, row * LANES : (row + 1) * LANES] / denom
        attended[own_row(row, rows // cores, cores)] = part.astype(jnp.bfloat16)


def product(tiles, w, row):
    return dot(jnp.concatenate([tile[row] for tile in tiles], axis=1), w[...])


def local_kernel(w, *refs):
    tiles, kept = refs[:-1], refs[-1]
    for row in range(kept.shape[0]):
        kept[row] = product(tiles, w, row)


def output_kernel(kept, *refs, tiles):
    parts, (out, staged, done) = refs[:-3], refs[-3:]
    groups = [parts[at : at + tiles + 1] for at in range(0, len(parts), tiles + 1)]
    copies = []
    for row in range(kept.shape[0]):
        total = kept[row]
        for group in groups:
            total = total + product(group[1:], group[0], row)
        staged[row] = total.astype(jnp.bfloat16)
        copies.append(pltpu.make_async_copy(staged.at[row], out.at[row], done.at[row]))
        copies[-1].start()
    for copy in copies:
        copy.wait()


def batches(blocks):
    every = tuple(range(CHUNKS))
    out = []
    for step in range(1, blocks):
        if step < blocks - 2:
            out.append((step, every))
        else:
            out += [(step, (k,)) for k in every if (step, k) != (blocks - 1, CHUNKS - 1)]
    return out


def shards(tokens, weights, key_mask, w_query, w_key, w_value, w_out):
    rows, cells, width = tokens.shape
    inner = w_query.shape[1]
    tiles = inner // LANES
    blocks = lax.axis_size("res")
    holders = lax.axis_size("seq")
    cores = lax.axis_size("head")
    part = HEAD_DIM
    share = rows // cores
    assert share * cores == rows and tiles * LANES == inner and part * CHUNKS == cells == LANES
    f32, bf16 = jnp.float32, jnp.bfloat16
    masked = MASKED / holders
    shape = pltpu.VMEM
    key_mask = key_mask.reshape(1, cells)

    length = share * part * width // LANES
    hbm = pl.BlockSpec(memory_space=pltpu.HBM)
    moving = [
        pl.pallas_call(
            functools.partial(pack_kernel, chunk=k, share=share),
            out_shape=shape((length + (0 if k else MARK_ROWS), LANES), bf16),
            in_specs=[hbm, hbm],
            out_specs=whole(1)[0],
            scratch_shapes=[
                shape((share, part, width), bf16),
                shape((1, cells), jnp.int32),
                pltpu.SemaphoreType.DMA((2,)),
            ],
            compiler_params=pltpu.CompilerParams(vmem_limit_bytes=VMEM_LIMIT),
        )(pltpu.with_memory_space_constraint(tokens, pltpu.HBM), pltpu.with_memory_space_constraint(key_mask, pltpu.HBM))
        for k in range(CHUNKS)
    ]
    moving[0], tokens, w_query, w_key, w_value, w_out = lax.optimization_barrier(
        (moving[0], tokens, w_query, w_key, w_value, w_out)
    )
    columns = width // cores
    w_parts = call(
        functools.partial(columns_kernel, cores=cores),
        [shape((inner, columns), bf16) for _ in range(cores)],
        [w_out],
        0,
    )
    w_parts = [w_parts[0]] + [ring(w_parts[k], "head", k) for k in range(1, cores)]
    counts = [weights]
    for k in range(1, holders):
        counts.append(ring(weights, "seq", k))

    def exchange(logits):
        return [logits] + [ring(logits, "seq", k) for k in range(1, holders)]

    depth = PER_TILE * part
    spans = rows * LANES
    query, logits, values = call(
        functools.partial(own_kernel, cores=cores, masked=masked),
        [
            shape((tiles, cells, spans), bf16),
            shape((CHUNKS, tiles, cells, depth), f32),
            shape((CHUNKS, tiles, depth, spans), bf16),
        ],
        counts + [key_mask, tokens, w_query, w_key, w_value],
        2 * rows * cells * inner * (3 * width + cells * PER_TILE),
        holders,
        [pltpu.VMEM((CHUNKS, tiles, depth, spans), bf16)],
    )
    units = [([exchange(logits)], values)]

    pieces, moved = {}, {}

    def shared_rows(value):
        return [value] + [ring(value, "head", j) for j in range(1, cores)]

    last, tail = blocks - 1, CHUNKS - 1
    fine = []
    for step in range(1, blocks):
        if step == last:
            size = moving[tail].shape[0] // (PARTS * PIECE) * PIECE
            fine = call(
                functools.partial(split_kernel, tiles=width // LANES),
                [shape((size, LANES), bf16) for _ in range(PARTS)],
                [moving[tail]],
                0,
            )
            fine = [ring(fine[n], "res") for n in range(PARTS)]
        count = tail if step == last else CHUNKS
        moving = [ring(moving[k], "res") for k in range(count)]
        moved[step] = moving[0]
        for k in range(count):
            pieces[step, k] = shared_rows(moving[k])

    def kernel(function, outs, args, rows, both, scratch_rows, high=part):
        return call(
            function,
            outs,
            args,
            2 * rows * part * inner * (both * width + cells * PER_TILE),
            0,
            [shape((1, tiles, PER_TILE * high, scratch_rows * LANES), bf16)] if scratch_rows else (),
        )

    for step, taken in batches(blocks):
        count = len(taken)
        logits_shape = shape((count, tiles, cells, depth), f32)
        values_shape = shape((count, tiles, depth, spans), bf16)
        if count > 1 or cores == 1:
            mine = sum([pieces[step, k] for k in taken], [])
            project = functools.partial(project_kernel, order=taken, masked=masked)
            logits, values = kernel(
                project, [logits_shape, values_shape], [query, w_key, w_value] + mine, rows * count, 2, rows
            )
            units.append(([exchange(logits)], values))
            continue
        mine, marks = pieces[step, taken[0]], moved[step]
        early = kernel(early_kernel, logits_shape, [query, w_key, mine[0]], share, 1, share)
        late = functools.partial(late_kernel, chunk=taken[0], masked=masked)
        logits = kernel(late, logits_shape, [query, w_key, marks, early] + mine[1:], rows - share, 1, rows - share)
        shared = exchange(logits)
        values = kernel(values_kernel, values_shape, [w_value] + mine, rows, 1, 0)
        units.append(([shared], values))

    tall = []
    for n, piece in enumerate(fine):
        logits_shape = shape((tiles, PER_TILE * PIECE, cells), f32)
        mine = shared_rows(piece)
        early = kernel(tall_early_kernel, logits_shape, [query, w_key, piece], share / 2, 1, share, PIECE)
        late = functools.partial(tall_late_kernel, first=tail * part + n * PIECE, masked=masked)
        logits = kernel(
            late,
            logits_shape,
            [query, w_key, moved[last], early] + mine[1:],
            (rows - share) / 2,
            1,
            rows - share,
            PIECE,
        )
        tall.append((exchange(logits), mine))
    if tall:
        values = kernel(
            tall_values_kernel,
            shape((1, tiles, depth, spans), bf16),
            [w_value] + sum([mine for _, mine in tall], []),
            rows,
            1,
            0,
        )
        units.append(([shared for shared, _ in tall], values))

    state = []
    state_shape = [
        shape((tiles, cells, LANES), f32),
        shape((tiles, cells, LANES), f32),
        shape((tiles, cells, spans), f32),
    ]

    def flatten(group):
        return sum([sum([list(piece) for piece in u[0]], []) + [u[1]] for u in group], [])

    def work(group):
        return sum(2 * cells * u[1].size for u in group)

    def sizes_of(group):
        return [(len(u[0]), len(u[0][0])) for u in group]

    cuts = groups_of(len(units))
    for cut in cuts[:-1]:
        group = units[slice(*cut)]
        state = call(
            functools.partial(absorb_kernel, sizes=sizes_of(group), carried=bool(state)),
            state_shape,
            flatten(group) + list(state),
            work(group),
        )
    group = units[slice(*cuts[-1])]
    attended, received = [], [[] for _ in range(1, cores)]
    for tile in range(tiles):
        finish = functools.partial(
            finish_kernel, sizes=sizes_of(group), carried=bool(state), cores=cores, tile=tile
        )
        attended.append(
            call(finish, shape((rows, cells, LANES), bf16), flatten(group) + list(state), work(group) / tiles)
        )
        for k in range(1, cores):
            received[k - 1].append(ring(attended[tile], "head", k))
    kept = call(
        local_kernel, shape((rows, cells, columns), f32), [w_parts[0]] + attended, 2 * rows * cells * inner * columns
    )
    others = sum([[w] + group for w, group in zip(w_parts[1:], received)], [])
    return pl.pallas_call(
        functools.partial(output_kernel, tiles=tiles),
        out_shape=pltpu.HBM((rows, cells, columns), bf16),
        in_specs=whole(1 + len(others)),
        out_specs=hbm,
        scratch_shapes=[shape((rows, cells, columns), bf16), pltpu.SemaphoreType.DMA((rows,))],
        compiler_params=pltpu.CompilerParams(vmem_limit_bytes=VMEM_LIMIT),
    )(kept, *others)


def groups_of(count):
    return [(at, min(at + 3, count - 1)) for at in range(0, count - 1, 3)] + [(count - 1, count)]


def solution(mesh):
    in_specs = (
        P(("grp", "seq"), "res", None),
        P(("grp", "seq")),
        P(("grp", "res")),
        P(None, "head"),
        P(None, "head"),
        P(None, "head"),
        P("head", None),
    )
    out_specs = P(("grp", "seq"), "res", "head")

    def placed(*args):
        step = jax.shard_map(shards, mesh=mesh, in_specs=in_specs, out_specs=out_specs, check_vma=False)
        return step(*args)

    return placed
```

```python
import functools
import math

import jax
import jax.numpy as jnp
from jax import lax
from jax.experimental import pallas as pl
from jax.experimental.pallas import tpu as pltpu
from jax.sharding import PartitionSpec as P


HEAD_DIM = 64
LANES = 128
PER_TILE = LANES // HEAD_DIM
CHUNKS = 2
MARK_ROWS = 8
PIECE = 32
PARTS = HEAD_DIM // PIECE
MASKED = -1000000000.0
VMEM_LIMIT = 24 * 1024 * 1024


def ring(value, axis, by=1):
    length = lax.axis_size(axis)
    return lax.ppermute(value, axis, [(i, (i + by) % length) for i in range(length)])


def whole(count):
    return [pl.BlockSpec(memory_space=pltpu.VMEM) for _ in range(count)]


def call(kernel, out_shape, args, flops, scalars=0, scratch=()):
    specs = [pl.BlockSpec(memory_space=pltpu.SMEM)] * scalars + whole(len(args) - scalars)
    multiple = isinstance(out_shape, (list, tuple))
    size = sum(a.size * a.dtype.itemsize for a in args)
    return pl.pallas_call(
        kernel,
        out_shape=out_shape,
        in_specs=specs,
        out_specs=whole(len(out_shape)) if multiple else whole(1)[0],
        scratch_shapes=list(scratch),
        cost_estimate=pl.CostEstimate(flops=int(flops), transcendentals=0, bytes_accessed=int(size)),
        compiler_params=pltpu.CompilerParams(vmem_limit_bytes=VMEM_LIMIT),
    )(*args)


def lane_head(shape):
    return lax.broadcasted_iota(jnp.int32, shape, len(shape) - 1) // HEAD_DIM


def dot(a, b):
    return jnp.dot(a, b, preferred_element_type=jnp.float32)


def dot_nt(a, b):
    return lax.dot_general(a, b, (((1,), (1,)), ((), ())), preferred_element_type=jnp.float32)


def tile_lanes(tile):
    return slice(tile * LANES, (tile + 1) * LANES)


def beside(flat, cells, tile):
    rows = flat.shape[0] // cells
    return jnp.concatenate(
        [flat[row * cells : (row + 1) * cells, tile_lanes(tile)] for row in range(rows)], axis=1
    )


def spread(target, chunk, flat, cells, first_row=0, first_cell=0):
    heads = lane_head((cells, LANES))
    for tile in range(flat.shape[1] // LANES):
        for row in range(flat.shape[0] // cells):
            part = flat[row * cells : (row + 1) * cells, tile_lanes(tile)]
            for h in range(PER_TILE):
                kept = jnp.where(heads == h, part, jnp.zeros_like(part))
                top = h * HEAD_DIM + first_cell
                target[chunk, tile, top : top + cells, tile_lanes(first_row + row)] = kept


def own_row(row, share, cores):
    core = lax.axis_index("head")
    return lax.rem(core + (cores - row // share), cores) * share + row % share


def live_rows(mask, first, count):
    cell = lax.broadcasted_iota(jnp.int32, (count, LANES), 0) + first
    here = cell == lax.broadcasted_iota(jnp.int32, (count, LANES), 1)
    marks = jnp.broadcast_to(mask[:1], (count, LANES))
    return jnp.max(jnp.where(here, marks, 0.0), axis=1, keepdims=True) > 0


def project(flat, w):
    return dot(flat, w[...]).astype(jnp.bfloat16)


def pack_kernel(tokens, mask, packed, landing, marks, done, *, chunk, share):
    _, part, width = landing.shape
    core = lax.axis_index("head")
    size = share * part
    used = width // LANES * size
    copies = [
        pltpu.make_async_copy(
            tokens.at[pl.ds(core * share, share), pl.ds(chunk * part, part)], landing, done.at[0]
        )
    ]
    if packed.shape[0] > used:
        copies.append(pltpu.make_async_copy(mask, marks, done.at[1]))
    for copy in copies:
        copy.start()
    for copy in copies:
        copy.wait()
    for tile in range(width // LANES):
        at = slice(tile * LANES, (tile + 1) * LANES)
        packed[tile * size : (tile + 1) * size] = landing[:, :, at].reshape(size, LANES)
    if packed.shape[0] > used:
        tail = packed.shape[0] - used
        packed[used:] = jnp.broadcast_to(marks[...].astype(jnp.float32), (tail, LANES)).astype(jnp.bfloat16)


def unpack(pieces, width):
    tiles = width // LANES
    flats = []
    for piece in pieces:
        size = piece.shape[0] // tiles // PIECE * PIECE
        flats.append(
            jnp.concatenate([piece[tile * size : (tile + 1) * size] for tile in range(tiles)], axis=1)
        )
    return jnp.concatenate(flats, axis=0)


def marks_of(piece):
    return piece[piece.shape[0] - MARK_ROWS :].astype(jnp.float32)


def project_kernel(query, w_key, w_value, *refs, order, masked):
    pieces, (logits, values) = refs[:-2], refs[-2:]
    per_chunk = len(pieces) // len(order)
    marks = marks_of(pieces[0])
    for at, chunk in enumerate(order):
        flat = unpack(pieces[at * per_chunk : (at + 1) * per_chunk], w_key.shape[0])
        keys = project(flat, w_key)
        live = live_rows(marks, chunk * HEAD_DIM, HEAD_DIM)
        for tile in range(query.shape[0]):
            total = dot_nt(beside(keys, HEAD_DIM, tile), query[tile])
            logits[tile, at * HEAD_DIM : (at + 1) * HEAD_DIM] = jnp.where(live, total, masked)
        spread(values, at, project(flat, w_value), HEAD_DIM)


def early_kernel(query, w_key, piece, logits):
    cells = logits.shape[1]
    keys = project(unpack([piece], w_key.shape[0]), w_key)
    width = keys.shape[0] // cells * LANES
    for tile in range(query.shape[0]):
        logits[tile] = dot_nt(beside(keys, cells, tile), query[tile, :, :width])


def late_kernel(query, w_key, marks, before, *refs, first, masked):
    pieces, logits = refs[:-1], refs[-1]
    cells = logits.shape[1]
    keys = project(unpack(pieces, w_key.shape[0]), w_key)
    live = live_rows(marks_of(marks), first, cells)
    skip = query.shape[2] - keys.shape[0] // cells * LANES
    for tile in range(query.shape[0]):
        total = before[tile] + dot_nt(beside(keys, cells, tile), query[tile, :, skip:])
        logits[tile] = jnp.where(live, total, masked)


def values_kernel(w_value, *refs, parts):
    pieces, values = refs[:-1], refs[-1]
    per_part = len(pieces) // parts
    cells = HEAD_DIM // parts
    for at in range(parts):
        flat = unpack(pieces[at * per_part : (at + 1) * per_part], w_value.shape[0])
        spread(values, 0, project(flat, w_value), cells, 0, at * cells)


def split_kernel(packed, *parts, tiles):
    size = packed.shape[0] // tiles
    count = len(parts)
    for at, part in enumerate(parts):
        for block in range(tiles * size // PIECE // count):
            source = (block * count + at) * PIECE
            part[block * PIECE : (block + 1) * PIECE] = packed[source : source + PIECE]


def own_kernel(*refs, cores, masked):
    counts, refs = refs[:-9], refs[-9:]
    mask, tokens, w_query, w_key, w_value, query, logits, values, keys = refs
    rows, cells, width = tokens.shape
    share = rows // cores
    tiles = query.shape[0]
    total = sum(count[row] for count in counts for row in range(rows))
    scale = lax.rsqrt(jnp.full((1, tiles * LANES), total, jnp.int32).astype(jnp.float32))
    heads = lane_head((cells, LANES))
    for part in range(cores):
        start = own_row(part * share, share, cores)
        block = tokens[pl.ds(start, share)].reshape(share * cells, width)
        asked = dot(block, w_query[...])
        key = project(block, w_key)
        value = project(block, w_value)
        for near in range(share):
            row = part * share + near
            at = slice(near * cells, (near + 1) * cells)
            count = jnp.full(scale.shape, counts[0][start + near], jnp.int32).astype(jnp.float32)
            factor = count * scale / math.sqrt(HEAD_DIM)
            scaled = (asked[at] * factor).astype(jnp.bfloat16)
            for tile in range(tiles):
                own = scaled[:, tile_lanes(tile)]
                keys[tile, :, tile_lanes(row)] = key[at, tile_lanes(tile)]
                for h in range(PER_TILE):
                    kept = jnp.where(heads == h, own, jnp.zeros_like(own))
                    query[tile, h * cells : (h + 1) * cells, tile_lanes(row)] = kept
            for chunk in range(CHUNKS):
                spread(values, chunk, value[at][chunk * HEAD_DIM : (chunk + 1) * HEAD_DIM], HEAD_DIM, row)
    live = live_rows(mask[...].astype(jnp.float32), 0, cells)
    for tile in range(tiles):
        logits[tile] = jnp.where(live, dot_nt(keys[tile], query[tile]), masked)


def upright(lines):
    return jnp.concatenate([jnp.broadcast_to(line, (HEAD_DIM, LANES)) for line in lines], axis=0).T


def absorb(units, state, tile, rows):
    scores, mixed = [[] for _ in range(PER_TILE)], []
    for pieces, values in units:
        totals = []
        for shared in pieces:
            total = shared[0][tile]
            for other in shared[1:]:
                total = total + other[tile]
            totals.append(total)
        total = jnp.concatenate(totals, axis=0) if len(totals) > 1 else totals[0]
        for chunk in range(values.shape[0]):
            for h in range(PER_TILE):
                scores[h].append(total[chunk * HEAD_DIM : (chunk + 1) * HEAD_DIM, tile_lanes(h)])
            mixed.append(values[chunk, tile])
    tops, denoms, expos, rescales = [], [], [], []
    for h in range(PER_TILE):
        top = jnp.max(functools.reduce(jnp.maximum, scores[h]), axis=0, keepdims=True)
        if state is not None:
            before = state[0][tile, h * 8 : h * 8 + 1]
            top = jnp.maximum(top, before)
            rescales.append(jnp.exp(before - top))
        expo = [jnp.exp(score - top) for score in scores[h]]
        denom = jnp.sum(functools.reduce(jnp.add, expo), axis=0, keepdims=True)
        if state is not None:
            denom = denom + state[1][tile, h * 8 : h * 8 + 1] * rescales[h]
        tops.append(top)
        denoms.append(denom)
        expos.append(expo)
    probs = []
    for chunk in range(len(mixed)):
        together = jnp.concatenate([expos[h][chunk] for h in range(PER_TILE)], axis=0)
        probs.append(together.T.astype(jnp.bfloat16))
    accum = dot(jnp.concatenate(probs, axis=1), jnp.concatenate(mixed, axis=0))
    if state is not None:
        accum = accum + state[2][tile] * jnp.concatenate([upright(rescales)] * rows, axis=1)
    return tops, denoms, accum


def read_units(refs, sizes):
    units, at = [], 0
    for parts, size in sizes:
        pieces = [refs[at + n * size : at + (n + 1) * size] for n in range(parts)]
        at += parts * size
        units.append((pieces, refs[at]))
        at += 1
    return units, refs[at:]


def absorb_kernel(*refs, sizes, carried):
    units, refs = read_units(refs, sizes)
    state = refs[:3] if carried else None
    top, denom, accum = refs[-3:]
    rows = accum.shape[2] // LANES
    for tile in range(accum.shape[0]):
        tops, denoms, accum[tile] = absorb(units, state, tile, rows)
        for h in range(PER_TILE):
            top[tile, h * 8 : h * 8 + 8] = jnp.broadcast_to(tops[h], (8, LANES))
            denom[tile, h * 8 : h * 8 + 8] = jnp.broadcast_to(denoms[h], (8, LANES))


def columns_of(w_out, ahead, cores):
    columns = w_out.shape[1] // cores
    at = lax.rem(lax.axis_index("head") + ahead, cores) * columns
    return w_out[:, pl.ds(pl.multiple_of(at, LANES), columns)]


def finish_kernel(*refs, sizes, carried, cores):
    units, refs = read_units(refs, sizes)
    state = refs[:3] if carried else None
    w_out, attended, sent = refs[-3:]
    rows, _, _ = attended.shape
    for tile in range(attended.shape[2] // LANES):
        _, denoms, accum = absorb(units, state, tile, rows)
        inverse = upright([1.0 / denom for denom in denoms])
        for row in range(rows):
            part = accum[:, tile_lanes(row)] * inverse
            attended[row, :, tile_lanes(tile)] = part.astype(jnp.bfloat16)
    write_output(attended, columns_of(w_out, 1 % cores, cores), sent, cores)


def write_output(attended, w, target, cores):
    rows, cells, inner = attended.shape
    share = rows // cores
    for part in range(cores):
        block = attended[part * share : (part + 1) * share].reshape(share * cells, inner)
        out = dot(block, w).astype(target.dtype).reshape(share, cells, w.shape[1])
        target[pl.ds(own_row(part * share, share, cores), share)] = out


def output_kernel(attended, w_out, kept, *, ahead, cores):
    write_output(attended, columns_of(w_out, ahead, cores), kept, cores)


def batches(blocks):
    every = tuple(range(CHUNKS))
    out = []
    for step in range(1, blocks):
        if step < blocks - 3:
            out.append((step, every))
        else:
            out += [(step, (k,)) for k in every if (step, k) != (blocks - 1, CHUNKS - 1)]
    return out


def shards(tokens, weights, key_mask, w_query, w_key, w_value, w_out):
    rows, cells, width = tokens.shape
    inner = w_query.shape[1]
    tiles = inner // LANES
    blocks = lax.axis_size("res")
    holders = lax.axis_size("seq")
    cores = lax.axis_size("head")
    part = HEAD_DIM
    share = rows // cores
    assert share * cores == rows and tiles * LANES == inner and part * CHUNKS == cells == LANES
    f32, bf16 = jnp.float32, jnp.bfloat16
    masked = MASKED / holders
    shape = pltpu.VMEM
    key_mask = key_mask.reshape(1, cells)

    length = share * part * width // LANES
    hbm = pl.BlockSpec(memory_space=pltpu.HBM)
    moving = [
        pl.pallas_call(
            functools.partial(pack_kernel, chunk=k, share=share),
            out_shape=shape((length + (0 if k else MARK_ROWS), LANES), bf16),
            in_specs=[hbm, hbm],
            out_specs=whole(1)[0],
            scratch_shapes=[
                shape((share, part, width), bf16),
                shape((1, cells), jnp.int32),
                pltpu.SemaphoreType.DMA((2,)),
            ],
            compiler_params=pltpu.CompilerParams(vmem_limit_bytes=VMEM_LIMIT),
        )(pltpu.with_memory_space_constraint(tokens, pltpu.HBM), pltpu.with_memory_space_constraint(key_mask, pltpu.HBM))
        for k in range(CHUNKS)
    ]
    counts = [weights]
    for k in range(1, holders):
        counts.append(ring(weights, "seq", k))

    def exchange(logits):
        return [logits] + [ring(logits, "seq", k) for k in range(1, holders)]

    depth = PER_TILE * part
    spans = rows * LANES
    query, logits, values = call(
        functools.partial(own_kernel, cores=cores, masked=masked),
        [
            shape((tiles, PER_TILE * cells, spans), bf16),
            shape((tiles, cells, PER_TILE * cells), f32),
            shape((CHUNKS, tiles, depth, spans), bf16),
        ],
        counts + [key_mask, tokens, w_query, w_key, w_value],
        2 * rows * cells * inner * (3 * width + cells * PER_TILE),
        holders,
        [shape((tiles, cells, spans), bf16)],
    )
    units = [([exchange(logits)], values)]

    pieces, moved = {}, {}

    def shared_rows(value):
        return [value] + [ring(value, "head", j) for j in range(1, cores)]

    last, tail = blocks - 1, CHUNKS - 1
    fine = []
    for step in range(1, blocks):
        if step == last:
            size = moving[tail].shape[0] // (PARTS * PIECE) * PIECE
            fine = call(
                functools.partial(split_kernel, tiles=width // LANES),
                [shape((size, LANES), bf16) for _ in range(PARTS)],
                [moving[tail]],
                0,
            )
            fine = [ring(fine[n], "res") for n in range(PARTS)]
        count = tail if step == last else CHUNKS
        moving = [ring(moving[k], "res") for k in range(count)]
        moved[step] = moving[0]
        for k in range(count):
            pieces[step, k] = shared_rows(moving[k])

    def kernel(function, outs, args, work):
        return call(function, outs, args, 2 * part * inner * work)

    def logits_shape(count):
        return shape((tiles, count, PER_TILE * cells), f32)

    def values_shape(count):
        return shape((count, tiles, depth, spans), bf16)

    def score_of(mine, marks, first, count):
        early = kernel(early_kernel, logits_shape(count), [query, w_key, mine[0]], width * share)
        late = functools.partial(late_kernel, first=first, masked=masked)
        args = [query, w_key, marks, early] + mine[1:]
        return exchange(kernel(late, logits_shape(count), args, width * share))

    def values_of(parts):
        function = functools.partial(values_kernel, parts=len(parts))
        return kernel(function, values_shape(1), [w_value] + sum(parts, []), width * rows)

    for step, taken in batches(blocks):
        count = len(taken)
        if count > 1 or cores == 1:
            outs = [logits_shape(count * part), values_shape(count)]
            args = [query, w_key, w_value] + sum([pieces[step, k] for k in taken], [])
            function = functools.partial(project_kernel, order=taken, masked=masked)
            logits, values = kernel(function, outs, args, 2 * count * width * rows)
            units.append(([exchange(logits)], values))
            continue
        mine = pieces[step, taken[0]]
        shared = score_of(mine, moved[step], taken[0] * part, part)
        units.append(([shared], values_of([mine])))

    tall = []
    for n, piece in enumerate(fine):
        mine = shared_rows(piece)
        tall.append((score_of(mine, moved[last], tail * part + n * PIECE, PIECE), mine))
    if tall:
        values = values_of([mine for _, mine in tall])
        units.append(([shared for shared, _ in tall], values))

    state = []
    state_shape = [
        shape((tiles, PER_TILE * 8, LANES), f32),
        shape((tiles, PER_TILE * 8, LANES), f32),
        shape((tiles, cells, spans), f32),
    ]

    def flatten(group):
        return sum([sum([list(piece) for piece in u[0]], []) + [u[1]] for u in group], [])

    def work(group):
        return sum(2 * cells * u[1].size for u in group)

    def sizes_of(group):
        return [(len(u[0]), len(u[0][0])) for u in group]

    cuts = groups_of(len(units))
    for cut in cuts[:-1]:
        group = units[slice(*cut)]
        state = call(
            functools.partial(absorb_kernel, sizes=sizes_of(group), carried=bool(state)),
            state_shape,
            flatten(group) + list(state),
            work(group),
        )
    group = units[slice(*cuts[-1])]
    columns = width // cores
    attended, sent = call(
        functools.partial(
            finish_kernel, sizes=sizes_of(group), carried=bool(state), cores=cores
        ),
        [shape((rows, cells, inner), bf16), shape((rows, cells, columns), bf16)],
        flatten(group) + list(state) + [w_out],
        work(group) + 2 * rows * cells * inner * columns,
    )

    def output(k):
        return call(
            functools.partial(output_kernel, ahead=k, cores=cores),
            shape((rows, cells, columns), f32),
            [attended, w_out],
            2 * rows * cells * inner * columns,
        )

    if cores == 1:
        return sent
    received = [ring(sent, "head")]
    for k in range(2, cores):
        received.append(ring(output(k).astype(bf16), "head", k))
    result = output(0)
    for value in received:
        result = result + value.astype(f32)
    return result.astype(bf16)


def groups_of(count):
    return [(at, min(at + 3, count - 1)) for at in range(0, count - 1, 3)] + [(count - 1, count)]


def solution(mesh):
    in_specs = (
        P(("grp", "seq"), "res", None),
        P(("grp", "seq")),
        P(("grp", "res")),
        P(None, "head"),
        P(None, "head"),
        P(None, "head"),
        P("head", None),
    )
    out_specs = P(("grp", "seq"), "res", "head")

    return jax.shard_map(shards, mesh=mesh, in_specs=in_specs, out_specs=out_specs, check_vma=False)
```

```python
import functools
import math

import jax
import jax.numpy as jnp
from jax import lax
from jax.experimental import pallas as pl
from jax.experimental.pallas import tpu as pltpu
from jax.sharding import PartitionSpec as P


HEAD_DIM = 64
LANES = 128
PER_TILE = LANES // HEAD_DIM
CHUNKS = 2
MARK_ROWS = 8
CLOSED = 0
PIECE = 32
PARTS = HEAD_DIM // PIECE
MASKED = -1000000000.0
VMEM_LIMIT = 24 * 1024 * 1024


def ring(value, axis, by=1):
    length = lax.axis_size(axis)
    return lax.ppermute(value, axis, [(i, (i + by) % length) for i in range(length)])


def pass_on(value):
    length = lax.axis_size("res")
    stops = list(range(length))
    if math.prod(lax.axis_size(axis) for axis in ("grp", "res", "seq", "head")) < CLOSED:
        stops = stops[::2] + stops[1::2][::-1]
    return lax.ppermute(value, "res", [(stops[i - 1], stops[i]) for i in range(length)])


def whole(count):
    return [pl.BlockSpec(memory_space=pltpu.VMEM) for _ in range(count)]


def call(kernel, out_shape, args, flops, scalars=0, scratch=()):
    specs = [pl.BlockSpec(memory_space=pltpu.SMEM)] * scalars + whole(len(args) - scalars)
    multiple = isinstance(out_shape, (list, tuple))
    size = sum(a.size * a.dtype.itemsize for a in args)
    return pl.pallas_call(
        kernel,
        out_shape=out_shape,
        in_specs=specs,
        out_specs=whole(len(out_shape)) if multiple else whole(1)[0],
        scratch_shapes=list(scratch),
        cost_estimate=pl.CostEstimate(flops=int(flops), transcendentals=0, bytes_accessed=int(size)),
        compiler_params=pltpu.CompilerParams(vmem_limit_bytes=VMEM_LIMIT),
    )(*args)


def lane_head(shape):
    return lax.broadcasted_iota(jnp.int32, shape, len(shape) - 1) // HEAD_DIM


def dot(a, b):
    return jnp.dot(a, b, preferred_element_type=jnp.float32)


def dot_nt(a, b):
    return lax.dot_general(a, b, (((1,), (1,)), ((), ())), preferred_element_type=jnp.float32)


def tile_lanes(tile):
    return slice(tile * LANES, (tile + 1) * LANES)


def beside(flat, cells, tile):
    rows = flat.shape[0] // cells
    return jnp.concatenate(
        [flat[row * cells : (row + 1) * cells, tile_lanes(tile)] for row in range(rows)], axis=1
    )


def spread(target, chunk, flat, cells, first_row=0, first_cell=0):
    heads = lane_head((cells, LANES))
    for tile in range(flat.shape[1] // LANES):
        for row in range(flat.shape[0] // cells):
            part = flat[row * cells : (row + 1) * cells, tile_lanes(tile)]
            for h in range(PER_TILE):
                kept = jnp.where(heads == h, part, jnp.zeros_like(part))
                top = h * HEAD_DIM + first_cell
                target[chunk, tile, top : top + cells, tile_lanes(first_row + row)] = kept


def own_row(row, share, cores):
    core = lax.axis_index("head")
    return lax.rem(core + (cores - row // share), cores) * share + row % share


def live_rows(mask, first, count):
    cell = lax.broadcasted_iota(jnp.int32, (count, LANES), 0) + first
    here = cell == lax.broadcasted_iota(jnp.int32, (count, LANES), 1)
    marks = jnp.broadcast_to(mask[:1], (count, LANES))
    return jnp.max(jnp.where(here, marks, 0.0), axis=1, keepdims=True) > 0


def project(flat, w):
    return dot(flat, w[...]).astype(jnp.bfloat16)


def pack_kernel(tokens, mask, packed, landing, marks, done, *, chunk, share):
    _, part, width = landing.shape
    core = lax.axis_index("head")
    size = share * part
    used = width // LANES * size
    copies = [
        pltpu.make_async_copy(
            tokens.at[pl.ds(core * share, share), pl.ds(chunk * part, part)], landing, done.at[0]
        )
    ]
    if packed.shape[0] > used:
        copies.append(pltpu.make_async_copy(mask, marks, done.at[1]))
    for copy in copies:
        copy.start()
    for copy in copies:
        copy.wait()
    for tile in range(width // LANES):
        at = slice(tile * LANES, (tile + 1) * LANES)
        packed[tile * size : (tile + 1) * size] = landing[:, :, at].reshape(size, LANES)
    if packed.shape[0] > used:
        tail = packed.shape[0] - used
        packed[used:] = jnp.broadcast_to(marks[...].astype(jnp.float32), (tail, LANES)).astype(jnp.bfloat16)


def unpack(pieces, width):
    tiles = width // LANES
    flats = []
    for piece in pieces:
        size = piece.shape[0] // tiles // PIECE * PIECE
        flats.append(
            jnp.concatenate([piece[tile * size : (tile + 1) * size] for tile in range(tiles)], axis=1)
        )
    return jnp.concatenate(flats, axis=0)


def marks_of(piece):
    return piece[piece.shape[0] - MARK_ROWS :].astype(jnp.float32)


def project_kernel(query, w_key, w_value, *refs, order, masked):
    pieces, (logits, values) = refs[:-2], refs[-2:]
    per_chunk = len(pieces) // len(order)
    marks = marks_of(pieces[0])
    for at, chunk in enumerate(order):
        flat = unpack(pieces[at * per_chunk : (at + 1) * per_chunk], w_key.shape[0])
        keys = project(flat, w_key)
        live = live_rows(marks, chunk * HEAD_DIM, HEAD_DIM)
        for tile in range(query.shape[0]):
            total = dot_nt(beside(keys, HEAD_DIM, tile), query[tile])
            logits[tile, at * HEAD_DIM : (at + 1) * HEAD_DIM] = jnp.where(live, total, masked)
        spread(values, at, project(flat, w_value), HEAD_DIM)


def early_kernel(query, w_key, piece, logits):
    cells = logits.shape[1]
    keys = project(unpack([piece], w_key.shape[0]), w_key)
    width = keys.shape[0] // cells * LANES
    for tile in range(query.shape[0]):
        logits[tile] = dot_nt(beside(keys, cells, tile), query[tile, :, :width])


def late_kernel(query, w_key, marks, before, *refs, first, masked):
    pieces, logits = refs[:-1], refs[-1]
    cells = logits.shape[1]
    keys = project(unpack(pieces, w_key.shape[0]), w_key)
    live = live_rows(marks_of(marks), first, cells)
    skip = query.shape[2] - keys.shape[0] // cells * LANES
    for tile in range(query.shape[0]):
        total = before[tile] + dot_nt(beside(keys, cells, tile), query[tile, :, skip:])
        logits[tile] = jnp.where(live, total, masked)


def values_kernel(w_value, *refs, parts):
    pieces, values = refs[:-1], refs[-1]
    per_part = len(pieces) // parts
    cells = HEAD_DIM // parts
    for at in range(parts):
        flat = unpack(pieces[at * per_part : (at + 1) * per_part], w_value.shape[0])
        spread(values, 0, project(flat, w_value), cells, 0, at * cells)


def split_kernel(packed, *parts, tiles):
    size = packed.shape[0] // tiles
    count = len(parts)
    for at, part in enumerate(parts):
        for block in range(tiles * size // PIECE // count):
            source = (block * count + at) * PIECE
            part[block * PIECE : (block + 1) * PIECE] = packed[source : source + PIECE]


def own_kernel(*refs, cores, masked):
    counts, refs = refs[:-9], refs[-9:]
    mask, tokens, w_query, w_key, w_value, query, logits, values, keys = refs
    rows, cells, width = tokens.shape
    share = rows // cores
    tiles = query.shape[0]
    total = sum(count[row] for count in counts for row in range(rows))
    scale = lax.rsqrt(jnp.full((1, tiles * LANES), total, jnp.int32).astype(jnp.float32))
    heads = lane_head((cells, LANES))
    for part in range(cores):
        start = own_row(part * share, share, cores)
        block = tokens[pl.ds(start, share)].reshape(share * cells, width)
        asked = dot(block, w_query[...])
        key = project(block, w_key)
        value = project(block, w_value)
        for near in range(share):
            row = part * share + near
            at = slice(near * cells, (near + 1) * cells)
            count = jnp.full(scale.shape, counts[0][start + near], jnp.int32).astype(jnp.float32)
            factor = count * scale / math.sqrt(HEAD_DIM)
            scaled = (asked[at] * factor).astype(jnp.bfloat16)
            for tile in range(tiles):
                own = scaled[:, tile_lanes(tile)]
                keys[tile, :, tile_lanes(row)] = key[at, tile_lanes(tile)]
                for h in range(PER_TILE):
                    kept = jnp.where(heads == h, own, jnp.zeros_like(own))
                    query[tile, h * cells : (h + 1) * cells, tile_lanes(row)] = kept
            for chunk in range(CHUNKS):
                spread(values, chunk, value[at][chunk * HEAD_DIM : (chunk + 1) * HEAD_DIM], HEAD_DIM, row)
    live = live_rows(mask[...].astype(jnp.float32), 0, cells)
    for tile in range(tiles):
        logits[tile] = jnp.where(live, dot_nt(keys[tile], query[tile]), masked)


def upright(lines):
    return jnp.concatenate([jnp.broadcast_to(line, (HEAD_DIM, LANES)) for line in lines], axis=0).T


def absorb(units, state, tile, rows):
    scores, mixed = [[] for _ in range(PER_TILE)], []
    for pieces, values in units:
        totals = []
        for shared in pieces:
            total = shared[0][tile]
            for other in shared[1:]:
                total = total + other[tile]
            totals.append(total)
        total = jnp.concatenate(totals, axis=0) if len(totals) > 1 else totals[0]
        for chunk in range(values.shape[0]):
            for h in range(PER_TILE):
                scores[h].append(total[chunk * HEAD_DIM : (chunk + 1) * HEAD_DIM, tile_lanes(h)])
            mixed.append(values[chunk, tile])
    tops, denoms, expos, rescales = [], [], [], []
    for h in range(PER_TILE):
        top = jnp.max(functools.reduce(jnp.maximum, scores[h]), axis=0, keepdims=True)
        if state is not None:
            before = state[0][tile, h * 8 : h * 8 + 1]
            top = jnp.maximum(top, before)
            rescales.append(jnp.exp(before - top))
        expo = [jnp.exp(score - top) for score in scores[h]]
        denom = jnp.sum(functools.reduce(jnp.add, expo), axis=0, keepdims=True)
        if state is not None:
            denom = denom + state[1][tile, h * 8 : h * 8 + 1] * rescales[h]
        tops.append(top)
        denoms.append(denom)
        expos.append(expo)
    probs = []
    for chunk in range(len(mixed)):
        together = jnp.concatenate([expos[h][chunk] for h in range(PER_TILE)], axis=0)
        probs.append(together.T.astype(jnp.bfloat16))
    accum = dot(jnp.concatenate(probs, axis=1), jnp.concatenate(mixed, axis=0))
    if state is not None:
        accum = accum + state[2][tile] * jnp.concatenate([upright(rescales)] * rows, axis=1)
    return tops, denoms, accum


def read_units(refs, sizes):
    units, at = [], 0
    for parts, size in sizes:
        pieces = [refs[at + n * size : at + (n + 1) * size] for n in range(parts)]
        at += parts * size
        units.append((pieces, refs[at]))
        at += 1
    return units, refs[at:]


def absorb_kernel(*refs, sizes, carried):
    units, refs = read_units(refs, sizes)
    state = refs[:3] if carried else None
    top, denom, accum = refs[-3:]
    rows = accum.shape[2] // LANES
    for tile in range(accum.shape[0]):
        tops, denoms, accum[tile] = absorb(units, state, tile, rows)
        for h in range(PER_TILE):
            top[tile, h * 8 : h * 8 + 8] = jnp.broadcast_to(tops[h], (8, LANES))
            denom[tile, h * 8 : h * 8 + 8] = jnp.broadcast_to(denoms[h], (8, LANES))


def columns_of(w_out, ahead, cores):
    columns = w_out.shape[1] // cores
    at = lax.rem(lax.axis_index("head") + ahead, cores) * columns
    return w_out[:, pl.ds(pl.multiple_of(at, LANES), columns)]


def finish_kernel(*refs, sizes, carried, cores):
    units, refs = read_units(refs, sizes)
    state = refs[:3] if carried else None
    w_out, attended, sent = refs[-3:]
    rows, _, _ = attended.shape
    for tile in range(attended.shape[2] // LANES):
        _, denoms, accum = absorb(units, state, tile, rows)
        inverse = upright([1.0 / denom for denom in denoms])
        for row in range(rows):
            part = accum[:, tile_lanes(row)] * inverse
            attended[row, :, tile_lanes(tile)] = part.astype(jnp.bfloat16)
    write_output(attended, columns_of(w_out, 1 % cores, cores), sent, cores)


def write_output(attended, w, target, cores):
    rows, cells, inner = attended.shape
    share = rows // cores
    for part in range(cores):
        block = attended[part * share : (part + 1) * share].reshape(share * cells, inner)
        out = dot(block, w).astype(target.dtype).reshape(share, cells, w.shape[1])
        target[pl.ds(own_row(part * share, share, cores), share)] = out


def output_kernel(attended, w_out, kept, *, ahead, cores):
    write_output(attended, columns_of(w_out, ahead, cores), kept, cores)


def batches(blocks):
    every = tuple(range(CHUNKS))
    out = []
    for step in range(1, blocks):
        if step < blocks - 3:
            out.append((step, every))
        else:
            out += [(step, (k,)) for k in every if (step, k) != (blocks - 1, CHUNKS - 1)]
    return out


def shards(tokens, weights, key_mask, w_query, w_key, w_value, w_out):
    rows, cells, width = tokens.shape
    inner = w_query.shape[1]
    tiles = inner // LANES
    blocks = lax.axis_size("res")
    holders = lax.axis_size("seq")
    cores = lax.axis_size("head")
    part = HEAD_DIM
    share = rows // cores
    assert share * cores == rows and tiles * LANES == inner and part * CHUNKS == cells == LANES
    f32, bf16 = jnp.float32, jnp.bfloat16
    masked = MASKED / holders
    shape = pltpu.VMEM
    key_mask = key_mask.reshape(1, cells)

    length = share * part * width // LANES
    hbm = pl.BlockSpec(memory_space=pltpu.HBM)
    moving = [
        pl.pallas_call(
            functools.partial(pack_kernel, chunk=k, share=share),
            out_shape=shape((length + (0 if k else MARK_ROWS), LANES), bf16),
            in_specs=[hbm, hbm],
            out_specs=whole(1)[0],
            scratch_shapes=[
                shape((share, part, width), bf16),
                shape((1, cells), jnp.int32),
                pltpu.SemaphoreType.DMA((2,)),
            ],
            compiler_params=pltpu.CompilerParams(vmem_limit_bytes=VMEM_LIMIT),
        )(pltpu.with_memory_space_constraint(tokens, pltpu.HBM), pltpu.with_memory_space_constraint(key_mask, pltpu.HBM))
        for k in range(CHUNKS)
    ]
    counts = [weights]
    for k in range(1, holders):
        counts.append(ring(weights, "seq", k))

    def exchange(logits):
        return [logits] + [ring(logits, "seq", k) for k in range(1, holders)]

    depth = PER_TILE * part
    spans = rows * LANES
    query, logits, values = call(
        functools.partial(own_kernel, cores=cores, masked=masked),
        [
            shape((tiles, PER_TILE * cells, spans), bf16),
            shape((tiles, cells, PER_TILE * cells), f32),
            shape((CHUNKS, tiles, depth, spans), bf16),
        ],
        counts + [key_mask, tokens, w_query, w_key, w_value],
        2 * rows * cells * inner * (3 * width + cells * PER_TILE),
        holders,
        [shape((tiles, cells, spans), bf16)],
    )
    units = [([exchange(logits)], values)]

    pieces, moved = {}, {}

    def shared_rows(value):
        return [value] + [ring(value, "head", j) for j in range(1, cores)]

    last, tail = blocks - 1, CHUNKS - 1
    fine = []
    for step in range(1, blocks):
        if step == last:
            size = moving[tail].shape[0] // (PARTS * PIECE) * PIECE
            fine = call(
                functools.partial(split_kernel, tiles=width // LANES),
                [shape((size, LANES), bf16) for _ in range(PARTS)],
                [moving[tail]],
                0,
            )
            fine = [pass_on(fine[n]) for n in range(PARTS)]
        count = tail if step == last else CHUNKS
        moving = [pass_on(moving[k]) for k in range(count)]
        moved[step] = moving[0]
        for k in range(count):
            pieces[step, k] = shared_rows(moving[k])

    def kernel(function, outs, args, work):
        return call(function, outs, args, 2 * part * inner * work)

    def logits_shape(count):
        return shape((tiles, count, PER_TILE * cells), f32)

    def values_shape(count):
        return shape((count, tiles, depth, spans), bf16)

    def score_of(mine, marks, first, count):
        early = kernel(early_kernel, logits_shape(count), [query, w_key, mine[0]], width * share)
        late = functools.partial(late_kernel, first=first, masked=masked)
        args = [query, w_key, marks, early] + mine[1:]
        return exchange(kernel(late, logits_shape(count), args, width * share))

    def values_of(parts):
        function = functools.partial(values_kernel, parts=len(parts))
        return kernel(function, values_shape(1), [w_value] + sum(parts, []), width * rows)

    for step, taken in batches(blocks):
        count = len(taken)
        if count > 1 or cores == 1:
            outs = [logits_shape(count * part), values_shape(count)]
            args = [query, w_key, w_value] + sum([pieces[step, k] for k in taken], [])
            function = functools.partial(project_kernel, order=taken, masked=masked)
            logits, values = kernel(function, outs, args, 2 * count * width * rows)
            units.append(([exchange(logits)], values))
            continue
        mine = pieces[step, taken[0]]
        shared = score_of(mine, moved[step], taken[0] * part, part)
        units.append(([shared], values_of([mine])))

    tall = []
    for n, piece in enumerate(fine):
        mine = shared_rows(piece)
        tall.append((score_of(mine, moved[last], tail * part + n * PIECE, PIECE), mine))
    if tall:
        values = values_of([mine for _, mine in tall])
        units.append(([shared for shared, _ in tall], values))

    state = []
    state_shape = [
        shape((tiles, PER_TILE * 8, LANES), f32),
        shape((tiles, PER_TILE * 8, LANES), f32),
        shape((tiles, cells, spans), f32),
    ]

    def flatten(group):
        return sum([sum([list(piece) for piece in u[0]], []) + [u[1]] for u in group], [])

    def work(group):
        return sum(2 * cells * u[1].size for u in group)

    def sizes_of(group):
        return [(len(u[0]), len(u[0][0])) for u in group]

    cuts = groups_of(len(units))
    for cut in cuts[:-1]:
        group = units[slice(*cut)]
        state = call(
            functools.partial(absorb_kernel, sizes=sizes_of(group), carried=bool(state)),
            state_shape,
            flatten(group) + list(state),
            work(group),
        )
    group = units[slice(*cuts[-1])]
    columns = width // cores
    attended, sent = call(
        functools.partial(
            finish_kernel, sizes=sizes_of(group), carried=bool(state), cores=cores
        ),
        [shape((rows, cells, inner), bf16), shape((rows, cells, columns), bf16)],
        flatten(group) + list(state) + [w_out],
        work(group) + 2 * rows * cells * inner * columns,
    )

    def output(k):
        return call(
            functools.partial(output_kernel, ahead=k, cores=cores),
            shape((rows, cells, columns), f32),
            [attended, w_out],
            2 * rows * cells * inner * columns,
        )

    if cores == 1:
        return sent
    received = [ring(sent, "head")]
    for k in range(2, cores):
        received.append(ring(output(k).astype(bf16), "head", k))
    result = output(0)
    for value in received:
        result = result + value.astype(f32)
    return result.astype(bf16)


def groups_of(count):
    return [(at, min(at + 3, count - 1)) for at in range(0, count - 1, 3)] + [(count - 1, count)]


def solution(mesh):
    in_specs = (
        P(("grp", "seq"), "res", None),
        P(("grp", "seq")),
        P(("grp", "res")),
        P(None, "head"),
        P(None, "head"),
        P(None, "head"),
        P("head", None),
    )
    out_specs = P(("grp", "seq"), "res", "head")

    return jax.shard_map(shards, mesh=mesh, in_specs=in_specs, out_specs=out_specs, check_vma=False)
```

```python
import functools
import math

import jax
import jax.numpy as jnp
from jax import lax
from jax.experimental import pallas as pl
from jax.experimental.pallas import tpu as pltpu
from jax.sharding import PartitionSpec as P


HEAD_DIM = 64
LANES = 128
PER_TILE = LANES // HEAD_DIM
CHUNKS = 2
MARK_ROWS = 8
CLOSED = 128
PIECE = 32
PARTS = HEAD_DIM // PIECE
MASKED = -1000000000.0
VMEM_LIMIT = 24 * 1024 * 1024


def ring(value, axis, by=1):
    length = lax.axis_size(axis)
    return lax.ppermute(value, axis, [(i, (i + by) % length) for i in range(length)])


def pass_on(value):
    length = lax.axis_size("res")
    stops = list(range(length))
    if math.prod(lax.axis_size(axis) for axis in ("grp", "res", "seq", "head")) < CLOSED:
        stops = stops[::2] + stops[1::2][::-1]
    return lax.ppermute(value, "res", [(stops[i], stops[i - 1]) for i in range(length)])


def whole(count):
    return [pl.BlockSpec(memory_space=pltpu.VMEM) for _ in range(count)]


def call(kernel, out_shape, args, flops, scalars=0, scratch=()):
    specs = [pl.BlockSpec(memory_space=pltpu.SMEM)] * scalars + whole(len(args) - scalars)
    multiple = isinstance(out_shape, (list, tuple))
    size = sum(a.size * a.dtype.itemsize for a in args)
    return pl.pallas_call(
        kernel,
        out_shape=out_shape,
        in_specs=specs,
        out_specs=whole(len(out_shape)) if multiple else whole(1)[0],
        scratch_shapes=list(scratch),
        cost_estimate=pl.CostEstimate(flops=int(flops), transcendentals=0, bytes_accessed=int(size)),
        compiler_params=pltpu.CompilerParams(vmem_limit_bytes=VMEM_LIMIT),
    )(*args)


def lane_head(shape):
    return lax.broadcasted_iota(jnp.int32, shape, len(shape) - 1) // HEAD_DIM


def dot(a, b):
    return jnp.dot(a, b, preferred_element_type=jnp.float32)


def dot_nt(a, b):
    return lax.dot_general(a, b, (((1,), (1,)), ((), ())), preferred_element_type=jnp.float32)


def tile_lanes(tile):
    return slice(tile * LANES, (tile + 1) * LANES)


def beside(flat, cells, tile):
    rows = flat.shape[0] // cells
    return jnp.concatenate(
        [flat[row * cells : (row + 1) * cells, tile_lanes(tile)] for row in range(rows)], axis=1
    )


def spread(target, chunk, flat, cells, first_row=0, first_cell=0):
    heads = lane_head((cells, LANES))
    for tile in range(flat.shape[1] // LANES):
        for row in range(flat.shape[0] // cells):
            part = flat[row * cells : (row + 1) * cells, tile_lanes(tile)]
            for h in range(PER_TILE):
                kept = jnp.where(heads == h, part, jnp.zeros_like(part))
                top = h * HEAD_DIM + first_cell
                target[chunk, tile, top : top + cells, tile_lanes(first_row + row)] = kept


def own_row(row, share, cores):
    core = lax.axis_index("head")
    return lax.rem(core + (cores - row // share), cores) * share + row % share


def live_rows(mask, first, count):
    cell = lax.broadcasted_iota(jnp.int32, (count, LANES), 0) + first
    here = cell == lax.broadcasted_iota(jnp.int32, (count, LANES), 1)
    marks = jnp.broadcast_to(mask[:1], (count, LANES))
    return jnp.max(jnp.where(here, marks, 0.0), axis=1, keepdims=True) > 0


def project(flat, w):
    return dot(flat, w[...]).astype(jnp.bfloat16)


def pack_kernel(tokens, mask, packed, landing, marks, done, *, chunk, share):
    _, part, width = landing.shape
    core = lax.axis_index("head")
    size = share * part
    used = width // LANES * size
    copies = [
        pltpu.make_async_copy(
            tokens.at[pl.ds(core * share, share), pl.ds(chunk * part, part)], landing, done.at[0]
        )
    ]
    if packed.shape[0] > used:
        copies.append(pltpu.make_async_copy(mask, marks, done.at[1]))
    for copy in copies:
        copy.start()
    for copy in copies:
        copy.wait()
    for tile in range(width // LANES):
        at = slice(tile * LANES, (tile + 1) * LANES)
        packed[tile * size : (tile + 1) * size] = landing[:, :, at].reshape(size, LANES)
    if packed.shape[0] > used:
        tail = packed.shape[0] - used
        packed[used:] = jnp.broadcast_to(marks[...].astype(jnp.float32), (tail, LANES)).astype(jnp.bfloat16)


def unpack(pieces, width):
    tiles = width // LANES
    flats = []
    for piece in pieces:
        size = piece.shape[0] // tiles // PIECE * PIECE
        flats.append(
            jnp.concatenate([piece[tile * size : (tile + 1) * size] for tile in range(tiles)], axis=1)
        )
    return jnp.concatenate(flats, axis=0)


def marks_of(piece):
    return piece[piece.shape[0] - MARK_ROWS :].astype(jnp.float32)


def project_kernel(query, w_key, w_value, marks, *refs, order, masked):
    pieces, (logits, values) = refs[:-2], refs[-2:]
    per_chunk = len(pieces) // len(order)
    marks = marks_of(marks)
    for at, chunk in enumerate(order):
        flat = unpack(pieces[at * per_chunk : (at + 1) * per_chunk], w_key.shape[0])
        keys = project(flat, w_key)
        live = live_rows(marks, chunk * HEAD_DIM, HEAD_DIM)
        for tile in range(query.shape[0]):
            total = dot_nt(beside(keys, HEAD_DIM, tile), query[tile])
            logits[tile, at * HEAD_DIM : (at + 1) * HEAD_DIM] = jnp.where(live, total, masked)
        spread(values, at, project(flat, w_value), HEAD_DIM)


def early_kernel(query, w_key, piece, logits):
    cells = logits.shape[1]
    keys = project(unpack([piece], w_key.shape[0]), w_key)
    width = keys.shape[0] // cells * LANES
    for tile in range(query.shape[0]):
        logits[tile] = dot_nt(beside(keys, cells, tile), query[tile, :, :width])


def late_kernel(query, w_key, marks, before, *refs, first, masked):
    pieces, logits = refs[:-1], refs[-1]
    cells = logits.shape[1]
    keys = project(unpack(pieces, w_key.shape[0]), w_key)
    live = live_rows(marks_of(marks), first, cells)
    skip = query.shape[2] - keys.shape[0] // cells * LANES
    for tile in range(query.shape[0]):
        total = before[tile] + dot_nt(beside(keys, cells, tile), query[tile, :, skip:])
        logits[tile] = jnp.where(live, total, masked)


def values_kernel(w_value, *refs, parts):
    pieces, values = refs[:-1], refs[-1]
    per_part = len(pieces) // parts
    cells = HEAD_DIM // parts
    for at in range(parts):
        flat = unpack(pieces[at * per_part : (at + 1) * per_part], w_value.shape[0])
        spread(values, 0, project(flat, w_value), cells, 0, at * cells)


def split_kernel(packed, *parts, tiles):
    size = packed.shape[0] // tiles
    count = len(parts)
    for at, part in enumerate(parts):
        for block in range(tiles * size // PIECE // count):
            source = (block * count + at) * PIECE
            part[block * PIECE : (block + 1) * PIECE] = packed[source : source + PIECE]


def own_kernel(*refs, cores, masked):
    counts, refs = refs[:-9], refs[-9:]
    mask, tokens, w_query, w_key, w_value, query, logits, values, keys = refs
    rows, cells, width = tokens.shape
    share = rows // cores
    tiles = query.shape[0]
    total = sum(count[row] for count in counts for row in range(rows))
    scale = lax.rsqrt(jnp.full((1, tiles * LANES), total, jnp.int32).astype(jnp.float32))
    heads = lane_head((cells, LANES))
    for part in range(cores):
        start = own_row(part * share, share, cores)
        block = tokens[pl.ds(start, share)].reshape(share * cells, width)
        asked = dot(block, w_query[...])
        key = project(block, w_key)
        value = project(block, w_value)
        for near in range(share):
            row = part * share + near
            at = slice(near * cells, (near + 1) * cells)
            count = jnp.full(scale.shape, counts[0][start + near], jnp.int32).astype(jnp.float32)
            factor = count * scale / math.sqrt(HEAD_DIM)
            scaled = (asked[at] * factor).astype(jnp.bfloat16)
            for tile in range(tiles):
                own = scaled[:, tile_lanes(tile)]
                keys[tile, :, tile_lanes(row)] = key[at, tile_lanes(tile)]
                for h in range(PER_TILE):
                    kept = jnp.where(heads == h, own, jnp.zeros_like(own))
                    query[tile, h * cells : (h + 1) * cells, tile_lanes(row)] = kept
            for chunk in range(CHUNKS):
                spread(values, chunk, value[at][chunk * HEAD_DIM : (chunk + 1) * HEAD_DIM], HEAD_DIM, row)
    live = live_rows(mask[...].astype(jnp.float32), 0, cells)
    for tile in range(tiles):
        logits[tile] = jnp.where(live, dot_nt(keys[tile], query[tile]), masked)


def upright(lines):
    return jnp.concatenate([jnp.broadcast_to(line, (HEAD_DIM, LANES)) for line in lines], axis=0).T


def absorb(units, state, tile, rows):
    scores, mixed = [[] for _ in range(PER_TILE)], []
    for pieces, values in units:
        totals = []
        for shared in pieces:
            total = shared[0][tile]
            for other in shared[1:]:
                total = total + other[tile]
            totals.append(total)
        total = jnp.concatenate(totals, axis=0) if len(totals) > 1 else totals[0]
        for chunk in range(values.shape[0]):
            for h in range(PER_TILE):
                scores[h].append(total[chunk * HEAD_DIM : (chunk + 1) * HEAD_DIM, tile_lanes(h)])
            mixed.append(values[chunk, tile])
    tops, denoms, expos, rescales = [], [], [], []
    for h in range(PER_TILE):
        top = jnp.max(functools.reduce(jnp.maximum, scores[h]), axis=0, keepdims=True)
        if state is not None:
            before = state[0][tile, h * 8 : h * 8 + 1]
            top = jnp.maximum(top, before)
            rescales.append(jnp.exp(before - top))
        expo = [jnp.exp(score - top) for score in scores[h]]
        denom = jnp.sum(functools.reduce(jnp.add, expo), axis=0, keepdims=True)
        if state is not None:
            denom = denom + state[1][tile, h * 8 : h * 8 + 1] * rescales[h]
        tops.append(top)
        denoms.append(denom)
        expos.append(expo)
    probs = []
    for chunk in range(len(mixed)):
        together = jnp.concatenate([expos[h][chunk] for h in range(PER_TILE)], axis=0)
        probs.append(together.T.astype(jnp.bfloat16))
    accum = dot(jnp.concatenate(probs, axis=1), jnp.concatenate(mixed, axis=0))
    if state is not None:
        accum = accum + state[2][tile] * jnp.concatenate([upright(rescales)] * rows, axis=1)
    return tops, denoms, accum


def read_units(refs, sizes):
    units, at = [], 0
    for parts, size in sizes:
        pieces = [refs[at + n * size : at + (n + 1) * size] for n in range(parts)]
        at += parts * size
        units.append((pieces, refs[at]))
        at += 1
    return units, refs[at:]


def absorb_kernel(*refs, sizes, carried):
    units, refs = read_units(refs, sizes)
    state = refs[:3] if carried else None
    top, denom, accum = refs[-3:]
    rows = accum.shape[2] // LANES
    for tile in range(accum.shape[0]):
        tops, denoms, accum[tile] = absorb(units, state, tile, rows)
        for h in range(PER_TILE):
            top[tile, h * 8 : h * 8 + 8] = jnp.broadcast_to(tops[h], (8, LANES))
            denom[tile, h * 8 : h * 8 + 8] = jnp.broadcast_to(denoms[h], (8, LANES))


def columns_of(w_out, ahead, cores):
    columns = w_out.shape[1] // cores
    at = lax.rem(lax.axis_index("head") + ahead, cores) * columns
    return w_out[:, pl.ds(pl.multiple_of(at, LANES), columns)]


def finish_kernel(*refs, sizes, carried, cores):
    units, refs = read_units(refs, sizes)
    state = refs[:3] if carried else None
    w_out, attended, sent = refs[-3:]
    rows, _, _ = attended.shape
    for tile in range(attended.shape[2] // LANES):
        _, denoms, accum = absorb(units, state, tile, rows)
        inverse = upright([1.0 / denom for denom in denoms])
        for row in range(rows):
            part = accum[:, tile_lanes(row)] * inverse
            attended[row, :, tile_lanes(tile)] = part.astype(jnp.bfloat16)
    write_output(attended, columns_of(w_out, 1 % cores, cores), sent, cores)


def write_output(attended, w, target, cores):
    rows, cells, inner = attended.shape
    share = rows // cores
    for part in range(cores):
        block = attended[part * share : (part + 1) * share].reshape(share * cells, inner)
        out = dot(block, w).astype(target.dtype).reshape(share, cells, w.shape[1])
        target[pl.ds(own_row(part * share, share, cores), share)] = out


def output_kernel(attended, w_out, kept, *, ahead, cores):
    write_output(attended, columns_of(w_out, ahead, cores), kept, cores)


def batches(blocks):
    every = tuple(range(CHUNKS))
    out = []
    for step in range(1, blocks):
        if step < blocks - 3:
            out.append((step, every))
        else:
            out += [(step, (k,)) for k in every if (step, k) != (blocks - 1, CHUNKS - 1)]
    return out


def shards(tokens, weights, key_mask, w_query, w_key, w_value, w_out):
    rows, cells, width = tokens.shape
    inner = w_query.shape[1]
    tiles = inner // LANES
    blocks = lax.axis_size("res")
    holders = lax.axis_size("seq")
    cores = lax.axis_size("head")
    part = HEAD_DIM
    share = rows // cores
    assert share * cores == rows and tiles * LANES == inner and part * CHUNKS == cells == LANES
    f32, bf16 = jnp.float32, jnp.bfloat16
    masked = MASKED / holders
    shape = pltpu.VMEM
    key_mask = key_mask.reshape(1, cells)

    length = share * part * width // LANES
    hbm = pl.BlockSpec(memory_space=pltpu.HBM)
    moving = [
        pl.pallas_call(
            functools.partial(pack_kernel, chunk=k, share=share),
            out_shape=shape((length + (0 if k else MARK_ROWS), LANES), bf16),
            in_specs=[hbm, hbm],
            out_specs=whole(1)[0],
            scratch_shapes=[
                shape((share, part, width), bf16),
                shape((1, cells), jnp.int32),
                pltpu.SemaphoreType.DMA((2,)),
            ],
            compiler_params=pltpu.CompilerParams(vmem_limit_bytes=VMEM_LIMIT),
        )(pltpu.with_memory_space_constraint(tokens, pltpu.HBM), pltpu.with_memory_space_constraint(key_mask, pltpu.HBM))
        for k in range(CHUNKS)
    ]
    counts = [weights]
    for k in range(1, holders):
        counts.append(ring(weights, "seq", k))

    def exchange(logits):
        return [logits] + [ring(logits, "seq", k) for k in range(1, holders)]

    depth = PER_TILE * part
    spans = rows * LANES
    query, logits, values = call(
        functools.partial(own_kernel, cores=cores, masked=masked),
        [
            shape((tiles, PER_TILE * cells, spans), bf16),
            shape((tiles, cells, PER_TILE * cells), f32),
            shape((CHUNKS, tiles, depth, spans), bf16),
        ],
        counts + [key_mask, tokens, w_query, w_key, w_value],
        2 * rows * cells * inner * (3 * width + cells * PER_TILE),
        holders,
        [shape((tiles, cells, spans), bf16)],
    )
    units = [([exchange(logits)], values)]

    pieces, moved = {}, {}

    def shared_rows(value):
        return [value] + [ring(value, "head", j) for j in range(1, cores)]

    last, tail = blocks - 1, CHUNKS - 1
    fine = []
    for step in range(1, blocks):
        if step == last:
            size = moving[tail].shape[0] // (PARTS * PIECE) * PIECE
            fine = call(
                functools.partial(split_kernel, tiles=width // LANES),
                [shape((size, LANES), bf16) for _ in range(PARTS)],
                [moving[tail]],
                0,
            )
            fine = [pass_on(fine[n]) for n in range(PARTS)]
        count = tail if step == last else CHUNKS
        moving = [pass_on(moving[k]) for k in range(count)]
        moved[step] = moving[0]
        for k in range(count):
            pieces[step, k] = shared_rows(moving[k])

    def kernel(function, outs, args, work):
        return call(function, outs, args, 2 * part * inner * work)

    def logits_shape(count):
        return shape((tiles, count, PER_TILE * cells), f32)

    def values_shape(count):
        return shape((count, tiles, depth, spans), bf16)

    def score_of(mine, marks, first, count):
        early = kernel(early_kernel, logits_shape(count), [query, w_key, mine[0]], width * share)
        late = functools.partial(late_kernel, first=first, masked=masked)
        args = [query, w_key, marks, early] + mine[1:]
        return exchange(kernel(late, logits_shape(count), args, width * share))

    def values_of(parts):
        function = functools.partial(values_kernel, parts=len(parts))
        return kernel(function, values_shape(1), [w_value] + sum(parts, []), width * rows)

    for step, taken in batches(blocks):
        count = len(taken)
        if step < last or cores == 1:
            outs = [logits_shape(count * part), values_shape(count)]
            args = [query, w_key, w_value, moved[step]] + sum([pieces[step, k] for k in taken], [])
            function = functools.partial(project_kernel, order=taken, masked=masked)
            logits, values = kernel(function, outs, args, 2 * count * width * rows)
            units.append(([exchange(logits)], values))
            continue
        mine = pieces[step, taken[0]]
        shared = score_of(mine, moved[step], taken[0] * part, part)
        units.append(([shared], values_of([mine])))

    tall = []
    for n, piece in enumerate(fine):
        mine = shared_rows(piece)
        tall.append((score_of(mine, moved[last], tail * part + n * PIECE, PIECE), mine))
    if tall:
        values = values_of([mine for _, mine in tall])
        units.append(([shared for shared, _ in tall], values))

    state = []
    state_shape = [
        shape((tiles, PER_TILE * 8, LANES), f32),
        shape((tiles, PER_TILE * 8, LANES), f32),
        shape((tiles, cells, spans), f32),
    ]

    def flatten(group):
        return sum([sum([list(piece) for piece in u[0]], []) + [u[1]] for u in group], [])

    def work(group):
        return sum(2 * cells * u[1].size for u in group)

    def sizes_of(group):
        return [(len(u[0]), len(u[0][0])) for u in group]

    cuts = groups_of(len(units))
    for cut in cuts[:-1]:
        group = units[slice(*cut)]
        state = call(
            functools.partial(absorb_kernel, sizes=sizes_of(group), carried=bool(state)),
            state_shape,
            flatten(group) + list(state),
            work(group),
        )
    group = units[slice(*cuts[-1])]
    columns = width // cores
    attended, sent = call(
        functools.partial(
            finish_kernel, sizes=sizes_of(group), carried=bool(state), cores=cores
        ),
        [shape((rows, cells, inner), bf16), shape((rows, cells, columns), bf16)],
        flatten(group) + list(state) + [w_out],
        work(group) + 2 * rows * cells * inner * columns,
    )

    def output(k):
        return call(
            functools.partial(output_kernel, ahead=k, cores=cores),
            shape((rows, cells, columns), f32),
            [attended, w_out],
            2 * rows * cells * inner * columns,
        )

    if cores == 1:
        return sent
    received = [ring(sent, "head")]
    for k in range(2, cores):
        received.append(ring(output(k).astype(bf16), "head", k))
    result = output(0)
    for value in received:
        result = result + value.astype(f32)
    return result.astype(bf16)


def groups_of(count):
    return [(at, min(at + 3, count - 1)) for at in range(0, count - 1, 3)] + [(count - 1, count)]


def solution(mesh):
    in_specs = (
        P(("grp", "seq"), "res", None),
        P(("grp", "seq")),
        P(("grp", "res")),
        P(None, "head"),
        P(None, "head"),
        P(None, "head"),
        P("head", None),
    )
    out_specs = P(("grp", "seq"), "res", "head")

    return jax.shard_map(shards, mesh=mesh, in_specs=in_specs, out_specs=out_specs, check_vma=False)
```
